512 devices in a mesh: ctx: 128 (over z, y, core), head: 4 (over x).
Axes of the slice: x: 4, y: 8, z: 8, core: 2. Of those that a mesh axis runs over, the one named last changes fastest.
Arguments:
- queries: bfloat16 [32768, 2048], P('ctx', 'head'), may hold values from -6 to 6
- keys: bfloat16 [32768, 2048], P('ctx', 'head'), may hold values from -6 to 6
- values: bfloat16 [32768, 2048], P('ctx', 'head'), may hold values from -6 to 6
- directions: bfloat16 [32768, 2048], P('ctx', 'head'), may hold values from -6 to 6
- rates: float32 [16, 32768], P('head', 'ctx'), may hold values from 0.004 to 1.996
- selected: int32 [256, 4], P('ctx'), may hold values from 0 to 255, as said below
- out_weight: bfloat16 [2048, 2048], P('head'), may hold values from -0.1875 to 0.1875
Outputs:
- projected: bfloat16 [32768, 2048], P('ctx', 'head')
The draws below stay inside these ranges and needn't reach their ends.
Inputs may be any that keep to these rules, and one draw needn't show every extreme that they name: `selected`: row c lists query block c's key blocks: entry 0 is c itself; the others lie from max(c - 14, 0) to c - 1 (or are 0 when c is 0), may repeat, and the farthest distance 7 * 2 is reached in every draw.
All inputs are finite; a program needn't handle non-finite values.
Results may differ from the reference program's by a relative error of at most 0.022.
Values may be sent and summed in bfloat16 or wider, within the bound.
A program may use at most 64 MiB of HBM per device.

```python
import math
import jax
import jax.numpy as jnp
from jax import lax

HEADS = 16
HEAD_DIM = 128
D = 2048
BLOCK = 128
TOPK = 4
LOOK = 7
TOK_DEV = 256
TOKENS = 32768
BLOCKS = 256
N_HEAD = 4


def query_key_pair(key):
    base = jax.random.fold_in(key, 7001)
    streams = jax.random.split(base, 2)
    shape = (TOKENS, HEADS, HEAD_DIM)
    query_all = jnp.clip(jax.random.normal(streams[0], shape, jnp.float32), -6.0, 6.0)
    key_all = jnp.clip(jax.random.normal(streams[1], shape, jnp.float32), -6.0, 6.0)
    return (query_all.reshape(TOKENS, HEADS * HEAD_DIM).astype(jnp.bfloat16), key_all.reshape(TOKENS, HEADS * HEAD_DIM).astype(jnp.bfloat16))


def draw_queries(key, part):
    return query_key_pair(key)[0]


def draw_keys(key, part):
    return query_key_pair(key)[1]


def draw_rates(key, part):
    streams = jax.random.split(jax.random.fold_in(key, 7002), 4)
    slow_share = 0.6
    slow = jax.random.uniform(streams[0], (HEADS, 1)) < slow_share
    spacing = jnp.exp(jax.random.uniform(streams[1], (HEADS, TOKENS), jnp.float32, math.log(0.004), math.log(0.12)))
    flipped = jax.random.uniform(streams[2], (HEADS, 1)) < 0.5
    slow_rate = jnp.where(flipped, 2.0 - spacing, spacing)
    fast_rate = jax.random.uniform(streams[3], (HEADS, TOKENS), jnp.float32, 0.3, 1.7)
    return jnp.where(slow, slow_rate, fast_rate).astype(jnp.float32)


def draw_selected(key, part):
    streams = jax.random.split(jax.random.fold_in(key, 7003), 2)
    reach_blocks = LOOK * (TOK_DEV // BLOCK)
    block_ids = jnp.arange(BLOCKS, dtype=jnp.int32)
    distance = jax.random.randint(streams[0], (BLOCKS, TOPK - 1), 1, reach_blocks + 1)
    farthest = (jax.random.randint(streams[1], (BLOCKS,), 0, 2) == 1) | (block_ids == BLOCKS - 1)
    first_col = jnp.where(farthest, reach_blocks, distance[:, 0])
    distance = jnp.concatenate([first_col[:, None], distance[:, 1:]], 1)
    picked = jnp.maximum(block_ids[:, None] - distance, 0)
    return jnp.concatenate([block_ids[:, None], picked], 1).astype(jnp.int32)


def with_spikes(entries, own_key, source, target, shards_of, factor):
    def block_of(dim):
        return (jnp.arange(entries.shape[dim]) // (entries.shape[dim] // shards_of)).reshape((-1,) + (1,) * (entries.ndim - 1 - dim))

    one_side = jax.random.permutation(own_key, shards_of)[block_of(target)]
    other_side = (block_of(target) + shards_of // 2) % shards_of
    return jnp.where((block_of(source) == one_side) | (block_of(source) == other_side), factor * entries, entries)


def shard_levels(key, shape, shards, low, largest):
    factor_of = 1.0
    for position, blocks in shards:
        draws = jax.random.uniform(jax.random.fold_in(jax.random.fold_in(key, 6), position), (blocks,), jnp.float32, low / len(shards), largest / len(shards))
        factor_of = factor_of * jnp.repeat(jnp.exp(draws), shape[position] // blocks).reshape((-1,) + (1,) * (len(shape) - 1 - position))
    return factor_of


def normal_values(rng, shape, deviation, most, pieces=(), kind=jnp.bfloat16):
    values = jax.random.normal(rng, shape, jnp.float32) * deviation
    if len(pieces) > 0:
        values = shard_levels(rng, shape, pieces, -0.22, 0.18) * values
    return jnp.clip(values, min=-most, max=most).astype(kind)


def heavy_noise(stream_key, dims, scale, reach, pieces, heavy, held_as=jnp.bfloat16):
    values = scale * jax.random.normal(stream_key, dims, jnp.float32)
    if pieces:
        values = values * shard_levels(stream_key, dims, pieces, -0.22, 0.18)
    return jnp.clip(with_spikes(values, jax.random.fold_in(stream_key, 3), *heavy), -reach, reach).astype(held_as)


def setup_inputs(seed: int = 0) -> dict:
    streams_of = jax.random.split(jax.random.key(seed), 8)
    return {
        "queries": draw_queries(jax.random.fold_in(streams_of[7], 71), 0),
        "keys": draw_keys(jax.random.fold_in(streams_of[7], 71), 0),
        "values": normal_values(streams_of[2], (TOKENS, HEADS * HEAD_DIM), 1.0, 6.0, ((0, 128), (1, 4))),
        "directions": normal_values(streams_of[3], (TOKENS, HEADS * HEAD_DIM), 1.0, 6.0, ((0, 128), (1, 4))),
        "rates": draw_rates(jax.random.fold_in(streams_of[7], 71), 0),
        "selected": draw_selected(jax.random.fold_in(streams_of[7], 71), 0),
        "out_weight": heavy_noise(streams_of[6], (HEADS * HEAD_DIM, D), (HEADS * HEAD_DIM) ** -0.5, 0.1875, ((0, 4),), (0, 1, 4, 2.0)),
    }


def product(left, right):
    return jnp.matmul(left, right, precision=lax.Precision.HIGHEST)

def flip_last(array):
    return jnp.swapaxes(array, -1, -2)

def block_terms(query_part, key_part, direction_part, rate_part):
    block_width = query_part.shape[-2]
    head_width = query_part.shape[-1]
    unit_vectors = direction_part * lax.rsqrt(lax.optimization_barrier(jnp.sum(direction_part * direction_part, -1, keepdims=True)) + 1e-06)
    positions = jnp.arange(block_width)
    strict_below = (positions[:, None] > positions[None, :]).astype(jnp.float32)
    at_or_below = (positions[:, None] >= positions[None, :]).astype(jnp.float32)
    identity = jnp.eye(block_width, dtype=jnp.float32)
    head_identity = jnp.eye(head_width, dtype=jnp.float32)
    gram_matrix = product(unit_vectors, flip_last(unit_vectors))
    lower_matrix = identity + rate_part[..., :, None] * gram_matrix * strict_below
    mixing = lax.linalg.triangular_solve(lower_matrix, rate_part[..., :, None] * identity, left_side=True, lower=True)
    query_proj = product(query_part, flip_last(unit_vectors)) * at_or_below
    key_proj = product(unit_vectors, flip_last(key_part)) * strict_below
    query_mix = product(query_proj, mixing)
    q_start = query_part - product(query_mix, unit_vectors)
    k_end = key_part - product(flip_last(product(mixing, key_proj)), unit_vectors)
    inner_scores = product(query_part, flip_last(key_part)) - product(query_mix, key_proj)
    block_maps = head_identity - product(product(flip_last(unit_vectors), mixing), unit_vectors)
    return (q_start, k_end, inner_scores, block_maps)

def reference(queries, keys, values, directions, rates, selected, out_weight):
    tokens = queries.shape[0]
    block_count = tokens // BLOCK
    score_scale = HEAD_DIM ** (-0.5)

    def blocked(array):
        return array.reshape(block_count, BLOCK, HEADS, HEAD_DIM).transpose(0, 2, 1, 3)
    query_blocks = blocked(queries).astype(jnp.float32)
    key_blocks = blocked(keys).astype(jnp.float32)
    direction_blocks = blocked(directions).astype(jnp.float32)
    value_blocks = blocked(values)
    rate_blocks = rates.reshape(HEADS, block_count, BLOCK).transpose(1, 0, 2)

    def one_block(packed):
        return block_terms(packed[0], packed[1], packed[2], packed[3])
    q_start, k_end, inner_scores, block_maps = lax.map(one_block, (query_blocks, key_blocks, direction_blocks, rate_blocks))
    reach_blocks = LOOK * (TOK_DEV // BLOCK)
    positions = jnp.arange(BLOCK)
    causal = (positions[:, None] >= positions[None, :])[None]

    def attend(query_block):
        listed = selected[query_block]
        score_list = [inner_scores[query_block] * score_scale]
        allowed_list = [causal & jnp.any(listed == query_block)]
        value_list = [value_blocks[query_block]]
        moving = q_start[query_block]
        for offset in range(1, reach_blocks + 1):
            earlier = query_block - offset
            source_block = jnp.maximum(earlier, 0)
            score_list.append(product(moving, flip_last(k_end[source_block])) * score_scale)
            hit = jnp.any(listed == earlier) & (earlier >= 0)
            allowed_list.append(jnp.broadcast_to(hit, (1, BLOCK, BLOCK)))
            value_list.append(value_blocks[source_block])
            moving = product(moving, block_maps[source_block])
        scores = jnp.concatenate(score_list, -1)
        allowed = jnp.concatenate(allowed_list, -1)
        highest = lax.optimization_barrier(jnp.max(jnp.where(allowed, scores, -1e+30), -1, keepdims=True))
        expos = jnp.exp(jnp.where(allowed, scores - highest, -1e+30))
        denominator = lax.optimization_barrier(jnp.sum(expos, -1, keepdims=True))
        weights = (expos / denominator).astype(jnp.bfloat16)
        values_all = jnp.concatenate(value_list, 1)
        blended = jnp.einsum('hqk,hke->hqe', weights.astype(jnp.float32), values_all.astype(jnp.float32))
        return blended.astype(jnp.bfloat16)
    attended = lax.map(attend, jnp.arange(block_count))
    attended_flat = attended.transpose(0, 2, 1, 3).reshape(tokens, HEADS * HEAD_DIM)
    group_width = HEADS * HEAD_DIM // N_HEAD
    summed = jnp.zeros((tokens, out_weight.shape[1]), jnp.float32)
    for group_index in range(N_HEAD):
        lo_col = group_index * group_width
        partial_value = jnp.dot(attended_flat[:, lo_col:lo_col + group_width].astype(jnp.float32), out_weight[lo_col:lo_col + group_width].astype(jnp.float32), preferred_element_type=jnp.float32)
        summed = summed + lax.optimization_barrier(partial_value.astype(jnp.bfloat16)).astype(jnp.float32)
    return summed.astype(jnp.bfloat16)
```

```python
import functools

import jax
import jax.numpy as jnp
from jax import lax
from jax.experimental import pallas as pl
from jax.experimental.pallas import tpu as pltpu
from jax.sharding import PartitionSpec as P

MESH = pl.DeviceIdType.MESH
HD = 128
B = 128
HEADS = 4
HOPS = 3
NEG = -1e30
SCALE = HD ** (-0.5)
f32 = jnp.float32
bf16 = jnp.bfloat16
NN = (((1,), (0,)), ((), ()))
NT = (((1,), (1,)), ((), ()))
TN = (((0,), (0,)), ((), ()))


def dot(a, b, dims):
    return lax.dot_general(a, b, dims, preferred_element_type=f32)


def split(a):
    high = a.astype(bf16)
    return high, (a - high.astype(f32)).astype(bf16)


def dot3(a, b, dims):
    return dot(a[0], b[0], dims) + (dot(a[1], b[0], dims) + dot(a[0], b[1], dims))


def dot_left(a, b, dims):
    return dot(a[0], b, dims) + dot(a[1], b, dims)


def dot_right(a, b, dims):
    return dot(a, b[0], dims) + dot(a, b[1], dims)


def block_terms(q, k, w, beta, hooks):
    each = range(len(q))
    row = lax.broadcasted_iota(jnp.int32, (B, B), 0)
    col = lax.broadcasted_iota(jnp.int32, (B, B), 1)
    eye = (row == col).astype(f32)
    grams = [
        dot(jnp.concatenate([w[i], q[i]], 0), jnp.concatenate([w[i], k[i]], 0), NT) for i in each
    ]
    wide = [w[i].astype(f32) for i in each]
    norm = [jnp.sum(wide[i] * wide[i], -1, keepdims=True) for i in each]
    rate = [
        jnp.transpose(jnp.broadcast_to(beta[i], (B, B))) / (norm[i] + 1e-6) for i in each
    ]
    lower = [jnp.where(row > col, rate[i] * grams[i][:B, :B], 0.0) for i in each]
    key_proj = [split(jnp.where(row > col, grams[i][:B, B:], 0.0)) for i in each]
    query_proj = [split(jnp.where(row >= col, grams[i][B:, :B], 0.0)) for i in each]

    def off_diagonal(size):
        return ((row ^ col) < 2 * size) & ((row & size) != 0) & ((col & size) == 0)

    inverse = [eye - jnp.where(off_diagonal(1), lower[i], 0.0) for i in each]
    size = 2
    while size < B:
        mask = off_diagonal(size)
        parts = [split(inverse[i]) for i in each]
        below = [split(jnp.where(mask, lower[i], 0.0)) for i in each]
        step = [split(dot3(below[i], parts[i], NN)) for i in each]
        inverse = [inverse[i] - dot3(parts[i], step[i], NN) for i in each]
        if size in hooks:
            hooks[size]()
        size *= 2
    mixing = [split(inverse[i] * jnp.transpose(rate[i])) for i in each]
    mix_w = [split(dot_left(mixing[i], w[i], NN)) for i in each]
    mix_k = [split(dot3(mixing[i], key_proj[i], NN)) for i in each]
    block_map = [eye - dot_right(w[i], mix_w[i], TN) for i in each]
    k_end = [k[i].astype(f32) - dot_left(mix_k[i], w[i], TN) for i in each]
    q_start = [q[i].astype(f32) - dot3(query_proj[i], mix_w[i], NN) for i in each]
    inner = [grams[i][B:, B:] - dot3(query_proj[i], mix_k[i], NN) for i in each]
    return q_start, k_end, inner, block_map


def kernel(
    n_ctx, sel, q_ref, k_ref, v_ref, w_ref, rate_ref, ow_ref, out_ref,
    k_own, k_par, k_ext, v_own, v_par, v_ext, k_stage, k_tail, d_mine, d_part,
    q_front, q_chip, m_ref, l_ref, acc_ref, local, att, wfull,
    sv, rv, svp, rvp, sve, rve, sk, rk, skp, rkp, ske, rke, sd, rd, sw, rw, swp, rwp, sa, ra, lw,
):
    me = lax.axis_index("ctx")
    x = lax.axis_index("head")
    core = lax.rem(me, 2)
    is0 = core == 0
    is1 = core == 1
    n_x = 4
    nxt = lax.rem(me + 2, n_ctx)
    prv = lax.rem(me + n_ctx - 2, n_ctx)
    partner = me + 1 - 2 * core
    cross = jnp.where(is0, lax.rem(me + n_ctx - 1, n_ctx), lax.rem(me + 1, n_ctx))
    lanes = [slice(h * HD, (h + 1) * HD) for h in range(HEADS)]
    rows = [slice(n * B, (n + 1) * B) for n in range(2)]

    def remote(src, dst, ss, rs, to):
        return pltpu.make_async_remote_copy(
            src_ref=src, dst_ref=dst, send_sem=ss, recv_sem=rs, device_id=to, device_id_type=MESH
        )

    barrier = pltpu.get_barrier_semaphore()
    for other in (nxt, prv, partner, cross):
        pl.semaphore_signal(barrier, inc=1, device_id=(other, x), device_id_type=MESH)
    for r in range(1, n_x):
        pl.semaphore_signal(
            barrier, inc=1, device_id=(me, lax.rem(x + r, n_x)), device_id_type=MESH
        )
    pl.semaphore_wait(barrier, 7)

    def v_hop(s, h):
        src = v_ref.at[:, lanes[h]] if s == 0 else v_own.at[s - 1, :, lanes[h]]
        return remote(src, v_own.at[s, :, lanes[h]], sv.at[s, h], rv.at[s, h], (nxt, x))

    def k_hop(s, h):
        return remote(
            k_stage.at[s, :, lanes[h]], k_own.at[s, :, lanes[h]], sk.at[s, h], rk.at[s, h], (nxt, x)
        )

    def v_share(s, h):
        return remote(
            v_own.at[s, :, lanes[h]], v_par.at[s, :, lanes[h]], svp.at[s, h], rvp.at[s, h], (partner, x)
        )

    def k_share(s, h):
        return remote(
            k_own.at[s, :, lanes[h]], k_par.at[s, :, lanes[h]], skp.at[s, h], rkp.at[s, h], (partner, x)
        )

    def v_extra(h, src, to):
        return remote(src.at[:, lanes[h]], v_ext.at[:, lanes[h]], sve.at[h], rve.at[h], (to, x))

    def k_extra(h, src, to):
        return remote(src.at[:, lanes[h]], k_ext.at[:, lanes[h]], ske.at[h], rke.at[h], (to, x))

    half = pl.ds(pl.multiple_of(core * 256, 256), 256)

    def w_send(r):
        to = lax.rem(x + r, n_x)
        cols = pl.ds(pl.multiple_of(to * 512, 512), 512)
        return remote(ow_ref.at[half, cols], wfull.at[x, half], sw.at[r - 1], rw.at[r - 1], (me, to))

    def w_recv(r):
        src = lax.rem(x + n_x - r, n_x)
        return remote(wfull.at[src, half], wfull.at[src, half], sw.at[r - 1], rw.at[r - 1], (me, src))

    def w_share(r):
        src = lax.rem(x + n_x - r, n_x)
        return remote(
            wfull.at[src, half], wfull.at[src, half], swp.at[r - 1], rwp.at[r - 1], (partner, x)
        )

    other_half = pl.ds(pl.multiple_of((1 - core) * 256, 256), 256)

    def w_shared(r):
        src = lax.rem(x + n_x - r, n_x)
        return remote(
            wfull.at[src, other_half], wfull.at[src, other_half], swp.at[r - 1], rwp.at[r - 1],
            (partner, x),
        )

    def a_send(r, h):
        to = lax.rem(x + r, n_x)
        slot = att.at[x, :, lanes[h]]
        return remote(slot, slot, sa.at[r - 1, h], ra.at[r - 1, h], (me, to))

    def a_recv(r, h):
        src = lax.rem(x + n_x - r, n_x)
        slot = att.at[src, :, lanes[h]]
        return remote(slot, slot, sa.at[r - 1, h], ra.at[r - 1, h], (me, src))

    own_w = pltpu.make_async_copy(
        ow_ref.at[:, pl.ds(pl.multiple_of(x * 512, 512), 512)], wfull.at[x], lw
    )

    for h in range(HEADS):
        v_hop(0, h).start()
    for r in range(1, n_x):
        w_send(r).start()
    own_w.start()

    @pl.when(is0)
    def _():
        for h in range(HEADS):
            v_extra(h, v_ref, partner).start()

    def pass_value(s, h):
        v_hop(s, h).wait_recv()
        v_share(s, h).start()
        if s < HOPS - 1:
            v_hop(s + 1, h).start()
        else:

            @pl.when(is1)
            def _():
                v_extra(h, v_own.at[HOPS - 1], cross).start()

    pairs = [(n, h) for h in range(HEADS) for n in range(2)]

    def cut(ref):
        return [ref[rows[n], lanes[h]] for n, h in pairs]

    hooks = {64: lambda: pass_value(0, 0)}
    q_start, k_end, inner, block_map = block_terms(
        cut(q_ref), cut(k_ref), cut(w_ref),
        [rate_ref[h : h + 1, rows[n]] for n, h in pairs], hooks,
    )
    maps = [split(m) for m in block_map]
    tails, fronts = [], []
    for h in range(HEADS):
        d_mine[:, lanes[h]] = dot3(maps[2 * h + 1], maps[2 * h], NN)
    exchange_d = remote(d_mine, d_part, sd, rd, (partner, x))
    exchange_d.start()
    for h in range(HEADS):
        first, second = 2 * h, 2 * h + 1
        early = split(k_end[first])
        tails.append(
            jnp.concatenate([dot3(early, maps[second], NT), k_end[second]], 0)
        )
        late = split(q_start[second])
        fronts.append(jnp.concatenate([q_start[first], dot3(late, maps[first], NN)], 0))
        q_front[:, lanes[h]] = (fronts[h] * SCALE).astype(bf16)
        k_tail[:, lanes[h]] = tails[h].astype(bf16)
        local[h, B:, :B] = dot3(late, early, NT) * SCALE
        local[h, :B, :B] = inner[first] * SCALE
        local[h, B:, B:] = inner[second] * SCALE

    @pl.when(is0)
    def _():
        for h in range(HEADS):
            k_extra(h, k_tail, partner).start()

    for h in range(1, HEADS):
        pass_value(0, h)
    exchange_d.wait_recv()
    chip_maps = []
    for h in range(HEADS):
        d_own = d_mine[:, lanes[h]]
        d_other = d_part[:, lanes[h]]
        other = split(d_other)
        carried = dot3(split(tails[h]), other, NT)
        k_stage[0, :, lanes[h]] = jnp.where(is0, carried, tails[h]).astype(bf16)
        k_hop(0, h).start()
        front = fronts[h]
        moved = dot3(split(front), other, NN)
        q_chip[:, lanes[h]] = (jnp.where(is0, front, moved) * SCALE).astype(bf16)
        later = jnp.where(is0, d_other, d_own)
        sooner = jnp.where(is0, d_own, d_other)
        chip_maps.append(split(dot3(split(later), split(sooner), NN)))

    def bias(n, block):
        hit = sel[n, 0] == block
        for e in range(1, 4):
            hit = hit | (sel[n, e] == block)
        return jnp.where(hit, 0.0, NEG).astype(f32)

    def first_block(h):
        row = lax.broadcasted_iota(jnp.int32, (B, B), 0)
        col = lax.broadcasted_iota(jnp.int32, (B, B), 1)
        for n in range(2):
            tiles = [local[h, rows[n], rows[b]] + bias(n, 2 * me + b) for b in range(n)]
            tiles.append(
                jnp.where(row >= col, local[h, rows[n], rows[n]] + bias(n, 2 * me + n), NEG)
            )
            top = functools.reduce(jnp.maximum, tiles)
            top = jnp.broadcast_to(jnp.max(top, -1, keepdims=True), (B, B))
            expos = [jnp.exp(t - top) for t in tiles]
            m_ref[h, rows[n], :] = top
            l_ref[h, rows[n], :] = functools.reduce(jnp.add, expos)
            total = jnp.zeros((B, HD), f32)
            for b, e in enumerate(expos):
                total = total + dot(e.astype(bf16), v_ref[rows[b], lanes[h]], NN)
            acc_ref[h, rows[n], :] = total

    def attend(h, query, sources):
        scores = [dot(query, keys, NT) for keys, _, _ in sources]
        for n in range(2):
            tiles = [
                scores[i][rows[n], rows[b]] + bias(n, 2 * device + b)
                for i, (_, _, device) in enumerate(sources)
                for b in range(2)
            ]
            old = m_ref[h, rows[n], :]
            top = functools.reduce(jnp.maximum, tiles)
            top = jnp.maximum(old, jnp.max(top, -1, keepdims=True))
            fade = jnp.exp(old - top)
            expos = [jnp.exp(t - top) for t in tiles]
            m_ref[h, rows[n], :] = top
            l_ref[h, rows[n], :] = l_ref[h, rows[n], :] * fade + functools.reduce(jnp.add, expos)
            total = acc_ref[h, rows[n], :] * fade
            for i, (_, values, _) in enumerate(sources):
                weights = jnp.concatenate(expos[2 * i : 2 * i + 2], 1).astype(bf16)
                total = total + dot(weights, values, NN)
            acc_ref[h, rows[n], :] = total

    def attend_extra(h):
        v_extra(h, v_own.at[HOPS - 1], cross).wait_recv()
        k_extra(h, k_tail, cross).wait_recv()
        device = jnp.where(is1, me - 1, me - 7)
        attend(h, q_front[:, lanes[h]], [(k_ext[:, lanes[h]], v_ext[:, lanes[h]], device)])

    def attend_hop(s, h):
        v_share(s, h).wait_recv()
        k_share(s, h).wait_recv()
        own = me - 2 * (s + 1)
        attend(
            h,
            q_chip[:, lanes[h]],
            [
                (k_own[s, :, lanes[h]], v_own[s, :, lanes[h]], own),
                (k_par[s, :, lanes[h]], v_par[s, :, lanes[h]], own + 1 - 2 * core),
            ],
        )

    def finish(h):
        total = jnp.sum(l_ref[h], -1, keepdims=True)
        att[x, :, lanes[h]] = (acc_ref[h] / total).astype(bf16)
        for r in range(1, n_x):
            a_send(r, h).start()

    def pass_key(s, h):
        k_hop(s, h).wait_recv()
        k_share(s, h).start()

        def forward():
            k_stage[s + 1, :, lanes[h]] = dot_right(k_own[s, :, lanes[h]], chip_maps[h], NT).astype(bf16)

        if s < HOPS - 1:
            forward()
            k_hop(s + 1, h).start()
        else:

            @pl.when(is1)
            def _():
                forward()
                k_extra(h, k_stage.at[HOPS], cross).start()

    for h in range(HEADS):
        first_block(h)

    @pl.when(is1)
    def _():
        for h in range(HEADS):
            attend_extra(h)

    for r in range(1, n_x):
        w_recv(r).wait_recv()
        w_share(r).start()
    for s in range(HOPS):
        if s + 1 < HOPS:
            for h in range(HEADS):
                pass_value(s + 1, h)
        for h in range(HEADS):
            pass_key(s, h)
        for h in range(HEADS):
            attend_hop(s, h)
            if s == HOPS - 1:

                @pl.when(is1)
                def _():
                    finish(h)

    @pl.when(is0)
    def _():
        for h in range(HEADS):
            attend_extra(h)
            finish(h)

    for r in range(1, n_x):
        w_shared(r).wait_recv()
    own_w.wait()
    total = dot(att[x], wfull[x], NN)
    for h in range(HEADS):
        for r in range(1, n_x):
            src = lax.rem(x + n_x - r, n_x)
            a_recv(r, h).wait_recv()
            total = total + dot(att[src, :, lanes[h]], wfull[src, lanes[h], :], NN)
    out_ref[...] = total.astype(bf16)

    exchange_d.wait_send()
    for r in range(1, n_x):
        w_send(r).wait_send()
        w_share(r).wait_send()
    for h in range(HEADS):
        for s in range(HOPS):
            v_hop(s, h).wait_send()
            k_hop(s, h).wait_send()
            v_share(s, h).wait_send()
            k_share(s, h).wait_send()
        v_extra(h, v_ref, partner).wait_send()
        k_extra(h, k_tail, partner).wait_send()
        for r in range(1, n_x):
            a_send(r, h).wait_send()


def solution(mesh):
    n_ctx = mesh.shape["ctx"]

    def body(queries, keys, values, directions, rates, selected, out_weight):
        tokens, width = queries.shape
        shard = (tokens, width)
        dma = pltpu.SemaphoreType.DMA
        vmem = pl.BlockSpec(memory_space=pltpu.VMEM)
        scratch = [
            pltpu.VMEM((HOPS,) + shard, bf16),
            pltpu.VMEM((HOPS,) + shard, bf16),
            pltpu.VMEM(shard, bf16),
            pltpu.VMEM((HOPS,) + shard, bf16),
            pltpu.VMEM((HOPS,) + shard, bf16),
            pltpu.VMEM(shard, bf16),
            pltpu.VMEM((HOPS + 1,) + shard, bf16),
            pltpu.VMEM(shard, bf16),
            pltpu.VMEM((HD, width), f32),
            pltpu.VMEM((HD, width), f32),
            pltpu.VMEM(shard, bf16),
            pltpu.VMEM(shard, bf16),
            pltpu.VMEM((HEADS, tokens, HD), f32),
            pltpu.VMEM((HEADS, tokens, HD), f32),
            pltpu.VMEM((HEADS, tokens, HD), f32),
            pltpu.VMEM((HEADS, tokens, tokens), f32),
            pltpu.VMEM((4,) + shard, bf16),
            pltpu.VMEM((4, width, width), bf16),
        ]
        hop, one = (HOPS, HEADS), (HEADS,)
        sems = [hop, hop, hop, hop, one, one] * 2 + [(), (), (3,), (3,), (3,), (3,), (3, HEADS), (3, HEADS), ()]
        scratch += [dma(s) if s else dma for s in sems]
        return pl.pallas_call(
            functools.partial(kernel, n_ctx),
            out_shape=jax.ShapeDtypeStruct(shard, bf16),
            in_specs=[
                pl.BlockSpec(memory_space=pltpu.SMEM),
                vmem, vmem, vmem, vmem, vmem,
                pl.BlockSpec(memory_space=pl.ANY),
            ],
            out_specs=vmem,
            scratch_shapes=scratch,
            compiler_params=pltpu.CompilerParams(
                collective_id=0, has_side_effects=True, vmem_limit_bytes=56 << 20
            ),
            name="path_attention",
        )(selected, queries, keys, values, directions, rates, out_weight)

    in_specs = (
        P("ctx", "head"),
        P("ctx", "head"),
        P("ctx", "head"),
        P("ctx", "head"),
        P("head", "ctx"),
        P("ctx", None),
        P("head", None),
    )
    return jax.shard_map(
        body, mesh=mesh, in_specs=in_specs, out_specs=P("ctx", "head"), check_vma=False
    )
```

```python
import functools

import jax
import jax.numpy as jnp
from jax import lax
from jax.experimental import pallas as pl
from jax.experimental.pallas import tpu as pltpu
from jax.sharding import PartitionSpec as P

MESH = pl.DeviceIdType.MESH
HD = 128
B = 128
HEADS = 4
NEG = -1e30
SCALE = HD ** (-0.5)
f32 = jnp.float32
bf16 = jnp.bfloat16
NN = (((1,), (0,)), ((), ()))
NT = (((1,), (1,)), ((), ()))
TN = (((0,), (0,)), ((), ()))


def dot(a, b, dims):
    return lax.dot_general(a, b, dims, preferred_element_type=f32)


def split(a):
    high = a.astype(bf16)
    return high, (a - high.astype(f32)).astype(bf16)


def dot3(a, b, dims):
    return dot(a[0], b[0], dims) + (dot(a[1], b[0], dims) + dot(a[0], b[1], dims))


def dot_left(a, b, dims):
    return dot(a[0], b, dims) + dot(a[1], b, dims)


def dot_right(a, b, dims):
    return dot(a, b[0], dims) + dot(a, b[1], dims)


def block_terms(q, k, w, beta):
    each = range(len(q))
    row = lax.broadcasted_iota(jnp.int32, (B, B), 0)
    col = lax.broadcasted_iota(jnp.int32, (B, B), 1)
    eye = (row == col).astype(f32)
    grams = [
        dot(jnp.concatenate([w[i], q[i]], 0), jnp.concatenate([w[i], k[i]], 0), NT) for i in each
    ]
    wide = [w[i].astype(f32) for i in each]
    norm = [jnp.sum(wide[i] * wide[i], -1, keepdims=True) for i in each]
    rate = [
        jnp.transpose(jnp.broadcast_to(beta[i], (B, B))) / (norm[i] + 1e-6) for i in each
    ]
    lower = [jnp.where(row > col, rate[i] * grams[i][:B, :B], 0.0) for i in each]
    key_proj = [split(jnp.where(row > col, grams[i][:B, B:], 0.0)) for i in each]
    query_proj = [split(jnp.where(row >= col, grams[i][B:, :B], 0.0)) for i in each]

    def off_diagonal(size):
        return ((row ^ col) < 2 * size) & ((row & size) != 0) & ((col & size) == 0)

    inverse = [eye - jnp.where(off_diagonal(1), lower[i], 0.0) for i in each]
    size = 2
    while size < B:
        mask = off_diagonal(size)
        parts = [split(inverse[i]) for i in each]
        below = [split(jnp.where(mask, lower[i], 0.0)) for i in each]
        step = [split(dot3(below[i], parts[i], NN)) for i in each]
        inverse = [inverse[i] - dot3(parts[i], step[i], NN) for i in each]
        size *= 2
    mixing = [split(inverse[i] * jnp.transpose(rate[i])) for i in each]
    mix_w = [split(dot_left(mixing[i], w[i], NN)) for i in each]
    mix_k = [split(dot3(mixing[i], key_proj[i], NN)) for i in each]
    block_map = [eye - dot_right(w[i], mix_w[i], TN) for i in each]
    k_end = [k[i].astype(f32) - dot_left(mix_k[i], w[i], TN) for i in each]
    q_start = [q[i].astype(f32) - dot3(query_proj[i], mix_w[i], NN) for i in each]
    inner = [grams[i][B:, B:] - dot3(query_proj[i], mix_k[i], NN) for i in each]
    return q_start, k_end, inner, block_map


def kernel(
    n_ctx, sel, q_ref, k_ref, v_ref, w_ref, rate_ref, ow_ref, out_ref,
    k_own, k_par, k_ext, v_own, v_par, v_ext, k_stage, k_tail, d_mine, d_part,
    q_front, q_home, q_in, q_vis, b_mine, b_in, o_out, o_in, s_out, s_in,
    m_ref, l_ref, acc_ref, local, att, wfull,
    sv, rv, svp, rvp, sve, rve, sk, rk, skp, rkp, ske, rke, sd, rd, sq, rq, sb, rb, so, ro, ss, rs,
    sw, rw, swp, rwp, sa, ra, sar, rar, lw,
):
    me = lax.axis_index("ctx")
    x = lax.axis_index("head")
    core = lax.rem(me, 2)
    is0 = core == 0
    is1 = core == 1
    n_x = 4
    nxt = lax.rem(me + 2, n_ctx)
    prv = lax.rem(me + n_ctx - 2, n_ctx)
    partner = me + 1 - 2 * core
    cross = jnp.where(is0, lax.rem(me + n_ctx - 1, n_ctx), lax.rem(me + 1, n_ctx))
    x_right = lax.rem(x + 1, n_x)
    x_left = lax.rem(x + n_x - 1, n_x)
    x_far = lax.rem(x + 2, n_x)
    has_next = me + 2 < n_ctx
    has_next2 = me + 4 < n_ctx
    has_prev = me >= 2
    has_prev2 = me >= 4
    crossed = (is0 & has_prev) | (is1 & has_next)
    feeds = is1 & has_prev & (me + 6 < n_ctx)
    visit1 = has_prev & has_next
    visit2 = has_prev & has_next2
    lanes = [slice(h * HD, (h + 1) * HD) for h in range(HEADS)]
    rows = [slice(n * B, (n + 1) * B) for n in range(2)]

    def remote(src, dst, send, recv, to):
        return pltpu.make_async_remote_copy(
            src_ref=src, dst_ref=dst, send_sem=send, recv_sem=recv, device_id=to, device_id_type=MESH
        )

    barrier = pltpu.get_barrier_semaphore()
    for other, there in ((nxt, has_next), (prv, has_prev), (cross, crossed)):

        @pl.when(there)
        def _():
            pl.semaphore_signal(barrier, inc=1, device_id=(other, x), device_id_type=MESH)

    pl.semaphore_signal(barrier, inc=1, device_id=(partner, x), device_id_type=MESH)
    for other in (x_right, x_far, x_left):
        pl.semaphore_signal(barrier, inc=1, device_id=(me, other), device_id_type=MESH)
    count = lambda flag: jnp.where(flag, 1, 0)
    pl.semaphore_wait(barrier, 4 + count(has_next) + count(has_prev) + count(crossed))

    def v_hop(h):
        return remote(v_ref.at[:, lanes[h]], v_own.at[:, lanes[h]], sv.at[h], rv.at[h], (nxt, x))

    def k_hop(h):
        return remote(
            k_stage.at[0, :, lanes[h]], k_own.at[:, lanes[h]], sk.at[h], rk.at[h], (nxt, x)
        )

    def v_share(h):
        return remote(
            v_own.at[:, lanes[h]], v_par.at[:, lanes[h]], svp.at[h], rvp.at[h], (partner, x)
        )

    def k_share(h):
        return remote(
            k_own.at[:, lanes[h]], k_par.at[:, lanes[h]], skp.at[h], rkp.at[h], (partner, x)
        )

    def v_extra(h, src, to):
        return remote(src.at[:, lanes[h]], v_ext.at[:, lanes[h]], sve.at[h], rve.at[h], (to, x))

    def k_extra(h, src, to):
        return remote(src.at[:, lanes[h]], k_ext.at[:, lanes[h]], ske.at[h], rke.at[h], (to, x))

    def q_hop(s, h):
        src = q_home.at[:, lanes[h]] if s == 0 else q_vis.at[0, :, lanes[h]]
        return remote(src, q_in.at[s, :, lanes[h]], sq.at[s, h], rq.at[s, h], (prv, x))

    def b_hop(s):
        src = b_mine if s == 0 else b_in.at[0]
        return remote(src, b_in.at[s], sb.at[s], rb.at[s], (prv, x))

    def o_hop(s, h):
        return remote(
            o_out.at[s, :, lanes[h]], o_in.at[s, :, lanes[h]], so.at[s, h], ro.at[s, h], (nxt, x)
        )

    def s_hop(s, h):
        return remote(s_out.at[s, h], s_in.at[s, h], ss.at[s, h], rs.at[s, h], (nxt, x))

    half = pl.ds(pl.multiple_of(core * 256, 256), 256)
    other_half = pl.ds(pl.multiple_of((1 - core) * 256, 256), 256)
    peers = [(x_right, x_left), (x_far, x_far), (x_left, x_right)]

    def w_send(r):
        to = peers[r][0]
        cols = pl.ds(pl.multiple_of(to * 512, 512), 512)
        return remote(ow_ref.at[half, cols], wfull.at[x, half], sw.at[r], rw.at[r], (me, to))

    def w_recv(r):
        src = peers[r][1]
        return remote(wfull.at[src, half], wfull.at[src, half], sw.at[r], rw.at[r], (me, src))

    def w_share(r, part):
        slot = wfull.at[peers[r][1], part]
        return remote(slot, slot, swp.at[r], rwp.at[r], (partner, x))

    def a_hop(r, h, owner, to):
        slot = att.at[owner, :, lanes[h]]
        return remote(slot, slot, sa.at[r, h], ra.at[r, h], (me, to))

    def a_relay(r, h, owner, to):
        slot = att.at[owner, rows[r], lanes[h]]
        return remote(slot, slot, sar.at[r, h], rar.at[r, h], (me, to))

    own_w = pltpu.make_async_copy(
        ow_ref.at[:, pl.ds(pl.multiple_of(x * 512, 512), 512)], wfull.at[x], lw
    )

    @pl.when(has_next)
    def _():
        for h in range(HEADS):
            v_hop(h).start()

    @pl.when(is0)
    def _():
        for h in range(HEADS):
            v_extra(h, v_ref, partner).start()

    for r in range(3):
        w_send(r).start()
    own_w.start()

    def bias(n, block):
        hit = sel[n, 0] == block
        for e in range(1, 4):
            hit = hit | (sel[n, e] == block)
        return jnp.where(hit, 0.0, NEG).astype(f32)

    away = [me - 4, me - 3 - 2 * core, me - 6, me - 5 - 2 * core, me - 7]
    for n in range(2):
        for i, device in enumerate(away):
            for b in range(2):
                line = 10 * n + 2 * i + b
                b_mine[line : line + 1, :] = jnp.full((1, HD), bias(n, 2 * device + b), f32)

    @pl.when(has_prev2)
    def _():
        b_hop(0).start()

    pairs = [(n, h) for h in range(HEADS) for n in range(2)]

    def cut(ref):
        return [ref[rows[n], lanes[h]] for n, h in pairs]

    q_start, k_end, inner, block_map = block_terms(
        cut(q_ref), cut(k_ref), cut(w_ref), [rate_ref[h : h + 1, rows[n]] for n, h in pairs]
    )
    maps = [split(m) for m in block_map]
    tails, fronts = [], []
    for h in range(HEADS):
        d_mine[:, lanes[h]] = dot3(maps[2 * h + 1], maps[2 * h], NN)
    exchange_d = remote(d_mine, d_part, sd, rd, (partner, x))
    exchange_d.start()
    for h in range(HEADS):
        first, second = 2 * h, 2 * h + 1
        early = split(k_end[first])
        tails.append(jnp.concatenate([dot3(early, maps[second], NT), k_end[second]], 0))
        late = split(q_start[second])
        fronts.append(jnp.concatenate([q_start[first], dot3(late, maps[first], NN)], 0))
        q_front[:, lanes[h]] = (fronts[h] * SCALE).astype(bf16)
        k_tail[:, lanes[h]] = tails[h].astype(bf16)
        local[h, B:, :B] = dot3(late, early, NT) * SCALE
        local[h, :B, :B] = inner[first] * SCALE
        local[h, B:, B:] = inner[second] * SCALE

    @pl.when(is0)
    def _():
        for h in range(HEADS):
            k_extra(h, k_tail, partner).start()

    @pl.when(has_prev)
    def _():
        for h in range(HEADS):
            v_hop(h).wait_recv()
            v_share(h).start()

            @pl.when(feeds)
            def _():
                v_extra(h, v_own, cross).start()

    exchange_d.wait_recv()
    chip_maps = []
    for h in range(HEADS):
        d_own = d_mine[:, lanes[h]]
        d_other = d_part[:, lanes[h]]
        other = split(d_other)
        carried = dot3(split(tails[h]), other, NT)
        k_stage[0, :, lanes[h]] = jnp.where(is0, carried, tails[h]).astype(bf16)
        moved = dot3(split(fronts[h]), other, NN)
        q_home[:, lanes[h]] = (jnp.where(is0, fronts[h], moved) * SCALE).astype(bf16)

        @pl.when(has_next)
        def _():
            k_hop(h).start()

        @pl.when(has_prev2)
        def _():
            q_hop(0, h).start()

        later = jnp.where(is0, d_other, d_own)
        sooner = jnp.where(is0, d_own, d_other)
        chip_maps.append(split(dot3(split(later), split(sooner), NN)))

    def first_block(h):
        row = lax.broadcasted_iota(jnp.int32, (B, B), 0)
        col = lax.broadcasted_iota(jnp.int32, (B, B), 1)
        for n in range(2):
            tiles = [local[h, rows[n], rows[b]] + bias(n, 2 * me + b) for b in range(n)]
            tiles.append(
                jnp.where(row >= col, local[h, rows[n], rows[n]] + bias(n, 2 * me + n), NEG)
            )
            top = functools.reduce(jnp.maximum, tiles)
            top = jnp.broadcast_to(jnp.max(top, -1, keepdims=True), (B, B))
            expos = [jnp.exp(t - top) for t in tiles]
            m_ref[h, rows[n], :] = top
            l_ref[h, rows[n], :] = functools.reduce(jnp.add, expos)
            total = jnp.zeros((B, HD), f32)
            for b, e in enumerate(expos):
                total = total + dot(e.astype(bf16), v_ref[rows[b], lanes[h]], NN)
            acc_ref[h, rows[n], :] = total

    def attend(g, query, sources, fresh=False):
        scores = [dot(query, keys, NT) for keys, _, _ in sources]
        for n in range(2):
            tiles = [
                scores[i][rows[n], rows[b]] + offset(n, b)
                for i, (_, _, offset) in enumerate(sources)
                for b in range(2)
            ]
            top = functools.reduce(jnp.maximum, tiles)
            top = jnp.broadcast_to(jnp.max(top, -1, keepdims=True), (B, B))
            if not fresh:
                old = m_ref[g, rows[n], :]
                top = jnp.maximum(old, top)
                fade = jnp.exp(old - top)
            expos = [jnp.exp(t - top) for t in tiles]
            norm = functools.reduce(jnp.add, expos)
            if not fresh:
                norm = norm + l_ref[g, rows[n], :] * fade
            m_ref[g, rows[n], :] = top
            l_ref[g, rows[n], :] = norm
            total = None if fresh else acc_ref[g, rows[n], :] * fade
            for i, (_, values, _) in enumerate(sources):
                weights = jnp.concatenate(expos[2 * i : 2 * i + 2], 1).astype(bf16)
                part = dot(weights, values, NN)
                total = part if total is None else total + part
            acc_ref[g, rows[n], :] = total

    def at_home(device):
        return lambda n, b: bias(n, 2 * device + b)

    def sent_along(s, i):
        def offset(n, b):
            line = 10 * n + 2 * i + b
            return b_in[s, line : line + 1, :]

        return offset

    def shards(h, own, other):
        return [
            (k_own[:, lanes[h]], v_own[:, lanes[h]], own),
            (k_par[:, lanes[h]], v_par[:, lanes[h]], other),
        ]

    def wait_extra(h):
        v_extra(h, v_own, cross).wait_recv()
        k_extra(h, k_tail, cross).wait_recv()

    def result(g):
        parts, logs = [], []
        for n in range(2):
            norm = jnp.sum(l_ref[g, rows[n], :], -1, keepdims=True)
            parts.append(acc_ref[g, rows[n], :] / norm)
            logs.append(jnp.transpose(m_ref[g, rows[n], :] + jnp.log(norm))[:1, :])
        return parts, logs

    def give(s, h):
        parts, logs = result((s + 1) * HEADS + h)
        for n in range(2):
            o_out[s, rows[n], lanes[h]] = parts[n].astype(bf16)
            s_out[s, h, n : n + 1, :] = logs[n]
        o_hop(s, h).start()
        s_hop(s, h).start()

    def take(s, h):
        o_hop(s, h).wait_recv()
        s_hop(s, h).wait_recv()
        g = s * HEADS + h
        for n in range(2):
            log = jnp.transpose(jnp.broadcast_to(s_in[s, h, n : n + 1, :], (B, B)))
            old = m_ref[g, rows[n], :]
            top = jnp.maximum(old, log)
            fade, weight = jnp.exp(old - top), jnp.exp(log - top)
            m_ref[g, rows[n], :] = top
            l_ref[g, rows[n], :] = l_ref[g, rows[n], :] * fade + weight * (1.0 / B)
            acc_ref[g, rows[n], :] = (
                acc_ref[g, rows[n], :] * fade + o_in[s, rows[n], lanes[h]].astype(f32) * weight
            )

    for h in range(HEADS):
        first_block(h)

    @pl.when(is1)
    def _():
        for h in range(HEADS):
            wait_extra(h)
            attend(h, q_front[:, lanes[h]], [(k_ext[:, lanes[h]], v_ext[:, lanes[h]], at_home(me - 1))])

    @pl.when(visit1)
    def _():
        b_hop(0).wait_recv()

        @pl.when(has_prev2)
        def _():
            b_hop(1).start()

    def wait_share(h):
        v_share(h).wait_recv()
        k_share(h).wait_recv()

    def near(h):
        device = me - 2
        attend(
            h,
            q_home[:, lanes[h]],
            shards(h, at_home(device), at_home(device + 1 - 2 * core)),
        )

        @pl.when(visit1)
        def _():
            attend(
                HEADS + h,
                q_vis[0, :, lanes[h]],
                shards(h, sent_along(0, 0), sent_along(0, 1)),
                fresh=True,
            )

    @pl.when(has_prev)
    def _():
        for h in range(HEADS):
            k_hop(h).wait_recv()
            k_share(h).start()

            @pl.when(feeds)
            def _():
                moved = dot_right(k_own[:, lanes[h]], chip_maps[h], NT)
                k_stage[1, :, lanes[h]] = moved.astype(bf16)
                k_extra(h, k_stage.at[1], cross).start()

            @pl.when(visit1)
            def _():
                q_hop(0, h).wait_recv()
                moved = dot_right(q_in[0, :, lanes[h]], chip_maps[h], NN)
                q_vis[0, :, lanes[h]] = moved.astype(bf16)

                @pl.when(has_prev2)
                def _():
                    q_hop(1, h).start()

            if h > 0:
                wait_share(h - 1)
                near(h - 1)
        wait_share(HEADS - 1)

    @pl.when(visit2)
    def _():
        b_hop(1).wait_recv()
        for h in range(HEADS):
            q_hop(1, h).wait_recv()
            moved = dot_right(q_in[1, :, lanes[h]], chip_maps[h], NN)
            q_vis[1, :, lanes[h]] = moved.astype(bf16)
            g = 2 * HEADS + h
            attend(
                g,
                q_vis[1, :, lanes[h]],
                shards(h, sent_along(1, 2), sent_along(1, 3)),
                fresh=True,
            )

            @pl.when(is0 & has_prev2)
            def _():
                wait_extra(h)
                attend(
                    g,
                    q_vis[1, :, lanes[h]],
                    [(k_ext[:, lanes[h]], v_ext[:, lanes[h]], sent_along(1, 4))],
                )

            give(1, h)

    for r in range(3):
        w_recv(r).wait_recv()
        w_share(r, half).start()

    @pl.when(has_prev)
    def _():
        near(HEADS - 1)

    @pl.when(visit1)
    def _():
        for h in range(HEADS):

            @pl.when(has_prev2)
            def _():
                take(1, h)

            give(0, h)

    def pass_head(h):
        a_hop(0, h, x_left, x_left).wait_recv()
        a_relay(0, h, x_left, x_right).start()
        a_hop(1, h, x_right, x_right).wait_recv()
        a_relay(1, h, x_right, x_left).start()

    for h in range(HEADS):

        @pl.when(has_prev2)
        def _():
            take(0, h)

        parts, _ = result(h)
        for n in range(2):
            att[x, rows[n], lanes[h]] = parts[n].astype(bf16)
        a_hop(0, h, x, x_right).start()
        a_hop(1, h, x, x_left).start()
        if h > 0:
            pass_head(h - 1)

    for r in range(3):
        w_share(r, other_half).wait_recv()
    own_w.wait()
    total = dot(att[x], wfull[x], NN)
    for h in range(HEADS):
        if h == HEADS - 1:
            pass_head(h)
        for src in (x_left, x_right):
            total = total + dot(att[src, :, lanes[h]], wfull[src, lanes[h], :], NN)
    for h in range(HEADS):
        a_relay(0, h, x_far, x_left).wait_recv()
        a_relay(1, h, x_far, x_right).wait_recv()
        total = total + dot(att[x_far, :, lanes[h]], wfull[x_far, lanes[h], :], NN)
    out_ref[...] = total.astype(bf16)

    exchange_d.wait_send()
    for r in range(3):
        w_send(r).wait_send()
        w_share(r, half).wait_send()
    for h in range(HEADS):
        a_hop(0, h, x, x_right).wait_send()
        a_hop(1, h, x, x_left).wait_send()
        a_relay(0, h, x_left, x_right).wait_send()
        a_relay(1, h, x_right, x_left).wait_send()

    @pl.when(has_next)
    def _():
        for h in range(HEADS):
            v_hop(h).wait_send()
            k_hop(h).wait_send()

    @pl.when(has_prev)
    def _():
        for h in range(HEADS):
            v_share(h).wait_send()
            k_share(h).wait_send()

    @pl.when(is0 | feeds)
    def _():
        for h in range(HEADS):
            v_extra(h, v_own, cross).wait_send()
            k_extra(h, k_tail, cross).wait_send()

    @pl.when(has_prev2)
    def _():
        b_hop(0).wait_send()
        for h in range(HEADS):
            q_hop(0, h).wait_send()

    @pl.when(visit1 & has_prev2)
    def _():
        b_hop(1).wait_send()
        for h in range(HEADS):
            q_hop(1, h).wait_send()

    for s, given in ((0, visit1), (1, visit2)):

        @pl.when(given)
        def _():
            for h in range(HEADS):
                o_hop(s, h).wait_send()
                s_hop(s, h).wait_send()


def solution(mesh):
    n_ctx = mesh.shape["ctx"]

    def body(queries, keys, values, directions, rates, selected, out_weight):
        tokens, width = queries.shape
        shard = (tokens, width)
        dma = pltpu.SemaphoreType.DMA
        vmem = pl.BlockSpec(memory_space=pltpu.VMEM)
        slab = pltpu.VMEM(shard, bf16)
        square = pltpu.VMEM((HD, width), f32)
        state = pltpu.VMEM((3 * HEADS, tokens, HD), f32)

        def pair(shape, dtype):
            return pltpu.VMEM((2,) + shape, dtype)

        scratch = [slab] * 6 + [pair(shard, bf16), slab, square, square]
        scratch += [slab, slab, pair(shard, bf16), pair(shard, bf16)]
        scratch += [pltpu.VMEM((20, HD), f32), pair((20, HD), f32)]
        scratch += [pair(shard, bf16), pair(shard, bf16)]
        scratch += [pair((HEADS, 2, HD), f32), pair((HEADS, 2, HD), f32)]
        scratch += [state, state, state, pltpu.VMEM((HEADS, tokens, tokens), f32)]
        scratch += [pltpu.VMEM((4,) + shard, bf16), pltpu.VMEM((4, width, width), bf16)]
        each, two = (HEADS,), (2, HEADS)
        sems = [each] * 12 + [(), (), two, two, (2,), (2,), two, two, two, two]
        sems += [(3,), (3,), (3,), (3,), two, two, two, two, ()]
        scratch += [dma(s) if s else dma for s in sems]
        return pl.pallas_call(
            functools.partial(kernel, n_ctx),
            out_shape=jax.ShapeDtypeStruct(shard, bf16),
            in_specs=[
                pl.BlockSpec(memory_space=pltpu.SMEM),
                vmem, vmem, vmem, vmem, vmem,
                pl.BlockSpec(memory_space=pl.ANY),
            ],
            out_specs=vmem,
            scratch_shapes=scratch,
            compiler_params=pltpu.CompilerParams(
                collective_id=0, has_side_effects=True, vmem_limit_bytes=56 << 20
            ),
            name="path_attention",
        )(selected, queries, keys, values, directions, rates, out_weight)

    in_specs = (
        P("ctx", "head"),
        P("ctx", "head"),
        P("ctx", "head"),
        P("ctx", "head"),
        P("head", "ctx"),
        P("ctx", None),
        P("head", None),
    )
    return jax.shard_map(
        body, mesh=mesh, in_specs=in_specs, out_specs=P("ctx", "head"), check_vma=False
    )
```

```python
import functools

import jax
import jax.numpy as jnp
from jax import lax
from jax.experimental import pallas as pl
from jax.experimental.pallas import tpu as pltpu
from jax.sharding import PartitionSpec as P

MESH = pl.DeviceIdType.MESH
HD = 128
B = 128
HEADS = 4
NEG = -1e30
PAUSE_AT = 4
SCALE = HD ** (-0.5)
f32 = jnp.float32
bf16 = jnp.bfloat16
NN = (((1,), (0,)), ((), ()))
NT = (((1,), (1,)), ((), ()))
TN = (((0,), (0,)), ((), ()))


def dot(a, b, dims):
    return lax.dot_general(a, b, dims, preferred_element_type=f32)


def split(a):
    high = a.astype(bf16)
    return high, (a - high.astype(f32)).astype(bf16)


def dot3(a, b, dims):
    return dot(a[0], b[0], dims) + (dot(a[1], b[0], dims) + dot(a[0], b[1], dims))


def dot_left(a, b, dims):
    return dot(a[0], b, dims) + dot(a[1], b, dims)


def dot_right(a, b, dims):
    return dot(a, b[0], dims) + dot(a, b[1], dims)


def block_terms(q, k, w, beta, pause, pause_at):
    each = range(len(q))
    row = lax.broadcasted_iota(jnp.int32, (B, B), 0)
    col = lax.broadcasted_iota(jnp.int32, (B, B), 1)
    eye = (row == col).astype(f32)
    grams = [
        dot(jnp.concatenate([w[i], q[i]], 0), jnp.concatenate([w[i], k[i]], 0), NT) for i in each
    ]
    wide = [w[i].astype(f32) for i in each]
    norm = [jnp.sum(wide[i] * wide[i], -1, keepdims=True) for i in each]
    rate = [
        jnp.transpose(jnp.broadcast_to(beta[i], (B, B))) / (norm[i] + 1e-6) for i in each
    ]
    lower = [jnp.where(row > col, rate[i] * grams[i][:B, :B], 0.0) for i in each]
    key_proj = [split(jnp.where(row > col, grams[i][:B, B:], 0.0)) for i in each]
    query_proj = [split(jnp.where(row >= col, grams[i][B:, :B], 0.0)) for i in each]

    def off_diagonal(size):
        return ((row ^ col) < 2 * size) & ((row & size) != 0) & ((col & size) == 0)

    inverse = [eye - jnp.where(off_diagonal(1), lower[i], 0.0) for i in each]
    size = 2
    while size < B:
        mask = off_diagonal(size)
        parts = [split(inverse[i]) for i in each]
        below = [split(jnp.where(mask, lower[i], 0.0)) for i in each]
        step = [split(dot3(below[i], parts[i], NN)) for i in each]
        inverse = [inverse[i] - dot3(parts[i], step[i], NN) for i in each]
        if size == pause_at:
            pause()
        size *= 2
    mixing = [split(inverse[i] * jnp.transpose(rate[i])) for i in each]
    mix_w = [split(dot_left(mixing[i], w[i], NN)) for i in each]
    mix_k = [split(dot3(mixing[i], key_proj[i], NN)) for i in each]
    block_map = [eye - dot_right(w[i], mix_w[i], TN) for i in each]
    k_end = [k[i].astype(f32) - dot_left(mix_k[i], w[i], TN) for i in each]
    q_start = [q[i].astype(f32) - dot3(query_proj[i], mix_w[i], NN) for i in each]
    inner = [grams[i][B:, B:] - dot3(query_proj[i], mix_k[i], NN) for i in each]
    return q_start, k_end, inner, block_map


def kernel(
    n_ctx, sel, q_hbm, k_hbm, v_hbm, w_hbm, rate_hbm, ow_ref, out_ref,
    q_ref, k_ref, v_ref, w_ref, rate_ref,
    k_own, k_par, k_ext, v_own, v_par, v_ext, k_stage, k_tail, d_mine, d_part,
    q_front, q_home, q_in, q_vis, b_mine, b_in, o_out, o_in, s_out, s_in,
    m_ref, l_ref, acc_ref, local, att, wfull,
    sv, rv, svp, rvp, sve, rve, sk, rk, skp, rkp, ske, rke, sd, rd, sq, rq, sb, rb, so, ro, ss, rs,
    sw, rw, swp, rwp, sa, ra, sar, rar, lw, li,
):
    me = lax.axis_index("ctx")
    x = lax.axis_index("head")
    core = lax.rem(me, 2)
    is0 = core == 0
    is1 = core == 1
    n_x = 4
    nxt = lax.rem(me + 2, n_ctx)
    prv = lax.rem(me + n_ctx - 2, n_ctx)
    partner = me + 1 - 2 * core
    cross = jnp.where(is0, lax.rem(me + n_ctx - 1, n_ctx), lax.rem(me + 1, n_ctx))
    x_right = lax.rem(x + 1, n_x)
    x_left = lax.rem(x + n_x - 1, n_x)
    x_far = lax.rem(x + 2, n_x)
    has_next = me + 2 < n_ctx
    has_next2 = me + 4 < n_ctx
    has_prev = me >= 2
    has_prev2 = me >= 4
    crossed = (is0 & has_prev) | (is1 & has_next)
    feeds = is1 & has_prev & (me + 6 < n_ctx)
    visit1 = has_prev & has_next
    visit2 = has_prev & has_next2
    lanes = [slice(h * HD, (h + 1) * HD) for h in range(HEADS)]
    rows = [slice(n * B, (n + 1) * B) for n in range(2)]

    def remote(src, dst, send, recv, to):
        return pltpu.make_async_remote_copy(
            src_ref=src, dst_ref=dst, send_sem=send, recv_sem=recv, device_id=to, device_id_type=MESH
        )

    barrier = pltpu.get_barrier_semaphore()
    for other, there in ((nxt, has_next), (prv, has_prev), (cross, crossed)):

        @pl.when(there)
        def _():
            pl.semaphore_signal(barrier, inc=1, device_id=(other, x), device_id_type=MESH)

    pl.semaphore_signal(barrier, inc=1, device_id=(partner, x), device_id_type=MESH)
    for other in (x_right, x_far, x_left):
        pl.semaphore_signal(barrier, inc=1, device_id=(me, other), device_id_type=MESH)
    count = lambda flag: jnp.where(flag, 1, 0)
    greetings = 4 + count(has_next) + count(has_prev) + count(crossed)
    inputs = [
        pltpu.make_async_copy(source, target, li.at[i])
        for i, (source, target) in enumerate(
            ((w_hbm, w_ref), (k_hbm, k_ref), (q_hbm, q_ref), (rate_hbm, rate_ref), (v_hbm, v_ref))
        )
    ]
    for copy in inputs:
        copy.start()

    def v_hop(h):
        return remote(v_hbm.at[:, lanes[h]], v_own.at[:, lanes[h]], sv.at[h], rv.at[h], (nxt, x))

    def k_hop(h):
        return remote(
            k_stage.at[0, :, lanes[h]], k_own.at[:, lanes[h]], sk.at[h], rk.at[h], (nxt, x)
        )

    def v_share(h):
        return remote(
            v_own.at[:, lanes[h]], v_par.at[:, lanes[h]], svp.at[h], rvp.at[h], (partner, x)
        )

    def k_share(h):
        return remote(
            k_own.at[:, lanes[h]], k_par.at[:, lanes[h]], skp.at[h], rkp.at[h], (partner, x)
        )

    def v_extra(h, src, to):
        return remote(src.at[:, lanes[h]], v_ext.at[:, lanes[h]], sve.at[h], rve.at[h], (to, x))

    def k_extra(h, src, to):
        return remote(src.at[:, lanes[h]], k_ext.at[:, lanes[h]], ske.at[h], rke.at[h], (to, x))

    def q_hop(s, h):
        src = q_home.at[:, lanes[h]] if s == 0 else q_vis.at[0, :, lanes[h]]
        return remote(src, q_in.at[s, :, lanes[h]], sq.at[s, h], rq.at[s, h], (prv, x))

    def b_hop(s):
        src = b_mine if s == 0 else b_in.at[0]
        return remote(src, b_in.at[s], sb.at[s], rb.at[s], (prv, x))

    def o_hop(s, h):
        return remote(
            o_out.at[s, :, lanes[h]], o_in.at[s, :, lanes[h]], so.at[s, h], ro.at[s, h], (nxt, x)
        )

    def s_hop(s, h):
        return remote(s_out.at[s, h], s_in.at[s, h], ss.at[s, h], rs.at[s, h], (nxt, x))

    half = pl.ds(pl.multiple_of(core * 256, 256), 256)
    other_half = pl.ds(pl.multiple_of((1 - core) * 256, 256), 256)
    peers = [(x_right, x_left), (x_far, x_far), (x_left, x_right)]

    def w_send(r):
        to = peers[r][0]
        cols = pl.ds(pl.multiple_of(to * 512, 512), 512)
        return remote(ow_ref.at[half, cols], wfull.at[x, half], sw.at[r], rw.at[r], (me, to))

    def w_recv(r):
        src = peers[r][1]
        return remote(wfull.at[src, half], wfull.at[src, half], sw.at[r], rw.at[r], (me, src))

    def w_share(r, part):
        slot = wfull.at[peers[r][1], part]
        return remote(slot, slot, swp.at[r], rwp.at[r], (partner, x))

    def a_hop(r, h, owner, to):
        slot = att.at[owner, :, lanes[h]]
        return remote(slot, slot, sa.at[r, h], ra.at[r, h], (me, to))

    def a_relay(r, h, owner, to):
        slot = att.at[owner, rows[r], lanes[h]]
        return remote(slot, slot, sar.at[r, h], rar.at[r, h], (me, to))

    own_w = pltpu.make_async_copy(
        ow_ref.at[:, pl.ds(pl.multiple_of(x * 512, 512), 512)], wfull.at[x], lw
    )

    def leave():
        pl.semaphore_wait(barrier, greetings)

        @pl.when(has_next)
        def _():
            for h in range(HEADS):
                v_hop(h).start()

        @pl.when(is0)
        def _():
            for h in range(HEADS):
                v_extra(h, v_hbm, partner).start()

        for r in range(3):
            w_send(r).start()
        own_w.start()

        @pl.when(has_prev2)
        def _():
            b_hop(0).start()

    def bias(n, block):
        hit = sel[n, 0] == block
        for e in range(1, 4):
            hit = hit | (sel[n, e] == block)
        return jnp.where(hit, 0.0, NEG).astype(f32)

    away = [me - 4, me - 3 - 2 * core, me - 6, me - 5 - 2 * core, jnp.where(is0, me - 7, -1)]
    for n in range(2):
        for i, device in enumerate(away):
            for b in range(2):
                line = 10 * n + 2 * i + b
                b_mine[line : line + 1, :] = jnp.full((1, HD), bias(n, 2 * device + b), f32)

    @pl.when(is0 & (me < 4))
    def _():
        k_ext[...] = jnp.zeros_like(k_ext)
        v_ext[...] = jnp.zeros_like(v_ext)

    pairs = [(n, h) for h in range(HEADS) for n in range(2)]

    def cut(ref):
        return [ref[rows[n], lanes[h]] for n, h in pairs]

    for copy in inputs[:4]:
        copy.wait()
    q_start, k_end, inner, block_map = block_terms(
        cut(q_ref), cut(k_ref), cut(w_ref), [rate_ref[h : h + 1, rows[n]] for n, h in pairs],
        leave, PAUSE_AT,
    )
    maps = [split(m) for m in block_map]
    tails, fronts = [], []
    for h in range(HEADS):
        d_mine[:, lanes[h]] = dot3(maps[2 * h + 1], maps[2 * h], NN)
    exchange_d = remote(d_mine, d_part, sd, rd, (partner, x))
    exchange_d.start()
    for h in range(HEADS):
        first, second = 2 * h, 2 * h + 1
        early = split(k_end[first])
        tails.append(jnp.concatenate([dot3(early, maps[second], NT), k_end[second]], 0))
        late = split(q_start[second])
        fronts.append(jnp.concatenate([q_start[first], dot3(late, maps[first], NN)], 0))
        q_front[:, lanes[h]] = (fronts[h] * SCALE).astype(bf16)
        k_tail[:, lanes[h]] = tails[h].astype(bf16)
        local[h, B:, :B] = dot3(late, early, NT) * SCALE
        local[h, :B, :B] = inner[first] * SCALE
        local[h, B:, B:] = inner[second] * SCALE

    @pl.when(is0)
    def _():
        for h in range(HEADS):
            k_extra(h, k_tail, partner).start()

    def pass_values(heads):
        @pl.when(has_prev)
        def _():
            for h in heads:
                v_hop(h).wait_recv()
                v_share(h).start()

    pass_values((0,))
    exchange_d.wait_recv()
    others = [split(d_part[:, lanes[h]]) for h in range(HEADS)]
    for h in range(HEADS):
        moved = dot3(split(fronts[h]), others[h], NN)
        q_home[:, lanes[h]] = (jnp.where(is0, fronts[h], moved) * SCALE).astype(bf16)

    @pl.when(has_prev2)
    def _():
        for h in range(HEADS):
            q_hop(0, h).start()

    for h in range(HEADS):
        carried = dot3(split(tails[h]), others[h], NT)
        k_stage[0, :, lanes[h]] = jnp.where(is0, carried, tails[h]).astype(bf16)

    @pl.when(has_next)
    def _():
        for h in range(HEADS):
            k_hop(h).start()

    chip_maps = []
    for h in range(HEADS):
        d_own = d_mine[:, lanes[h]]
        d_other = d_part[:, lanes[h]]
        later = jnp.where(is0, d_other, d_own)
        sooner = jnp.where(is0, d_own, d_other)
        chip_maps.append(split(dot3(split(later), split(sooner), NN)))
    pass_values((1, 2, 3))

    def first_block(h):
        row = lax.broadcasted_iota(jnp.int32, (B, B), 0)
        col = lax.broadcasted_iota(jnp.int32, (B, B), 1)
        for n in range(2):
            tiles = [local[h, rows[n], rows[b]] + bias(n, 2 * me + b) for b in range(n)]
            tiles.append(
                jnp.where(row >= col, local[h, rows[n], rows[n]] + bias(n, 2 * me + n), NEG)
            )
            top = functools.reduce(jnp.maximum, tiles)
            top = jnp.broadcast_to(jnp.max(top, -1, keepdims=True), (B, B))
            expos = [jnp.exp(t - top) for t in tiles]
            m_ref[h, rows[n], :] = top
            l_ref[h, rows[n], :] = functools.reduce(jnp.add, expos)
            total = jnp.zeros((B, HD), f32)
            for b, e in enumerate(expos):
                total = total + dot(e.astype(bf16), v_ref[rows[b], lanes[h]], NN)
            acc_ref[h, rows[n], :] = total

    def attend(g, query, sources, fresh=False):
        scores = [dot(query, keys, NT) for keys, _, _ in sources]
        for n in range(2):
            tiles = [
                scores[i][rows[n], rows[b]] + offset(n, b)
                for i, (_, _, offset) in enumerate(sources)
                for b in range(2)
            ]
            top = functools.reduce(jnp.maximum, tiles)
            top = jnp.broadcast_to(jnp.max(top, -1, keepdims=True), (B, B))
            if not fresh:
                old = m_ref[g, rows[n], :]
                top = jnp.maximum(old, top)
                fade = jnp.exp(old - top)
            expos = [jnp.exp(t - top) for t in tiles]
            norm = functools.reduce(jnp.add, expos)
            if not fresh:
                norm = norm + l_ref[g, rows[n], :] * fade
            m_ref[g, rows[n], :] = top
            l_ref[g, rows[n], :] = norm
            total = None if fresh else acc_ref[g, rows[n], :] * fade
            for i, (_, values, _) in enumerate(sources):
                weights = jnp.concatenate(expos[2 * i : 2 * i + 2], 1).astype(bf16)
                part = dot(weights, values, NN)
                total = part if total is None else total + part
            acc_ref[g, rows[n], :] = total

    def at_home(device):
        return lambda n, b: bias(n, 2 * device + b)

    def sent_along(s, i):
        def offset(n, b):
            line = 10 * n + 2 * i + b
            return b_in[s, line : line + 1, :]

        return offset

    def shards(h, own, other):
        return [
            (k_own[:, lanes[h]], v_own[:, lanes[h]], own),
            (k_par[:, lanes[h]], v_par[:, lanes[h]], other),
        ]

    def wait_extra(h):
        v_extra(h, v_own, cross).wait_recv()
        k_extra(h, k_tail, cross).wait_recv()

    def result(g):
        parts, logs = [], []
        for n in range(2):
            norm = jnp.sum(l_ref[g, rows[n], :], -1, keepdims=True)
            parts.append(acc_ref[g, rows[n], :] / norm)
            logs.append(jnp.transpose(m_ref[g, rows[n], :] + jnp.log(norm))[:1, :])
        return parts, logs

    def give(s, h):
        parts, logs = result((s + 1) * HEADS + h)
        for n in range(2):
            o_out[s, rows[n], lanes[h]] = parts[n].astype(bf16)
            s_out[s, h, n : n + 1, :] = logs[n]
        o_hop(s, h).start()
        s_hop(s, h).start()

    def take(s, h):
        o_hop(s, h).wait_recv()
        s_hop(s, h).wait_recv()
        g = s * HEADS + h
        for n in range(2):
            log = jnp.transpose(jnp.broadcast_to(s_in[s, h, n : n + 1, :], (B, B)))
            old = m_ref[g, rows[n], :]
            top = jnp.maximum(old, log)
            fade, weight = jnp.exp(old - top), jnp.exp(log - top)
            m_ref[g, rows[n], :] = top
            l_ref[g, rows[n], :] = l_ref[g, rows[n], :] * fade + weight * (1.0 / B)
            acc_ref[g, rows[n], :] = (
                acc_ref[g, rows[n], :] * fade + o_in[s, rows[n], lanes[h]].astype(f32) * weight
            )

    inputs[4].wait()
    for h in range(HEADS):
        first_block(h)

    @pl.when(is1)
    def _():
        for h in range(HEADS):
            wait_extra(h)
            attend(h, q_front[:, lanes[h]], [(k_ext[:, lanes[h]], v_ext[:, lanes[h]], at_home(me - 1))])

    @pl.when(visit1)
    def _():
        b_hop(0).wait_recv()

        @pl.when(has_prev2)
        def _():
            b_hop(1).start()

    def wait_share(h):
        v_share(h).wait_recv()
        k_share(h).wait_recv()

    def near(h):
        device = me - 2
        attend(
            h,
            q_home[:, lanes[h]],
            shards(h, at_home(device), at_home(device + 1 - 2 * core)),
        )
        attend(
            HEADS + h,
            q_vis[0, :, lanes[h]],
            shards(h, sent_along(0, 0), sent_along(0, 1)),
            fresh=True,
        )

    @pl.when(has_prev)
    def _():
        for h in range(HEADS):
            k_hop(h).wait_recv()
            k_share(h).start()

            @pl.when(feeds)
            def _():
                moved = dot_right(k_own[:, lanes[h]], chip_maps[h], NT)
                k_stage[1, :, lanes[h]] = moved.astype(bf16)
                k_extra(h, k_stage.at[1], cross).start()
                v_extra(h, v_own, cross).start()

            @pl.when(visit1)
            def _():
                q_hop(0, h).wait_recv()
                moved = dot_right(q_in[0, :, lanes[h]], chip_maps[h], NN)
                q_vis[0, :, lanes[h]] = moved.astype(bf16)

                @pl.when(has_prev2)
                def _():
                    q_hop(1, h).start()

            if h > 0:
                wait_share(h - 1)
                near(h - 1)
        wait_share(HEADS - 1)

    def far(h):
        @pl.when(visit2)
        def _():
            q_hop(1, h).wait_recv()
            moved = dot_right(q_in[1, :, lanes[h]], chip_maps[h], NN)
            q_vis[1, :, lanes[h]] = moved.astype(bf16)

            @pl.when(is0 & has_prev2)
            def _():
                wait_extra(h)

            attend(
                2 * HEADS + h,
                q_vis[1, :, lanes[h]],
                shards(h, sent_along(1, 2), sent_along(1, 3))
                + [(k_ext[:, lanes[h]], v_ext[:, lanes[h]], sent_along(1, 4))],
                fresh=True,
            )
            give(1, h)

    def back(h):
        @pl.when(visit1)
        def _():
            @pl.when(has_prev2)
            def _():
                take(1, h)

            give(0, h)

    @pl.when(visit2)
    def _():
        b_hop(1).wait_recv()

    far(0)
    far(1)
    far(2)

    @pl.when(has_prev)
    def _():
        near(HEADS - 1)

    for r in range(3):
        w_recv(r).wait_recv()
        w_share(r, half).start()
    back(0)
    far(3)
    back(1)
    back(2)

    def pass_head(h):
        a_hop(0, h, x_left, x_left).wait_recv()
        a_relay(0, h, x_left, x_right).start()
        a_hop(1, h, x_right, x_right).wait_recv()
        a_relay(1, h, x_right, x_left).start()

    def finish(h):
        @pl.when(has_prev2)
        def _():
            take(0, h)

        parts, _ = result(h)
        for n in range(2):
            att[x, rows[n], lanes[h]] = parts[n].astype(bf16)
        a_hop(0, h, x, x_right).start()
        a_hop(1, h, x, x_left).start()

    finish(0)
    back(3)
    finish(1)
    finish(2)
    pass_head(0)
    finish(3)
    pass_head(1)

    for r in range(3):
        w_share(r, other_half).wait_recv()
    own_w.wait()
    total = dot(att[x], wfull[x], NN)

    def near_part(total, h):
        for src in (x_left, x_right):
            total = total + dot(att[src, :, lanes[h]], wfull[src, lanes[h], :], NN)
        return total

    pass_head(2)
    total = near_part(near_part(total, 0), 1)
    pass_head(3)
    total = near_part(near_part(total, 2), 3)
    for h in range(HEADS):
        a_relay(0, h, x_far, x_left).wait_recv()
        a_relay(1, h, x_far, x_right).wait_recv()
        total = total + dot(att[x_far, :, lanes[h]], wfull[x_far, lanes[h], :], NN)
    out_ref[...] = total.astype(bf16)

    exchange_d.wait_send()
    for r in range(3):
        w_send(r).wait_send()
        w_share(r, half).wait_send()
    for h in range(HEADS):
        a_hop(0, h, x, x_right).wait_send()
        a_hop(1, h, x, x_left).wait_send()
        a_relay(0, h, x_left, x_right).wait_send()
        a_relay(1, h, x_right, x_left).wait_send()

    @pl.when(has_next)
    def _():
        for h in range(HEADS):
            v_hop(h).wait_send()
            k_hop(h).wait_send()

    @pl.when(has_prev)
    def _():
        for h in range(HEADS):
            v_share(h).wait_send()
            k_share(h).wait_send()

    @pl.when(is0 | feeds)
    def _():
        for h in range(HEADS):
            v_extra(h, v_own, cross).wait_send()
            k_extra(h, k_tail, cross).wait_send()

    @pl.when(has_prev2)
    def _():
        b_hop(0).wait_send()
        for h in range(HEADS):
            q_hop(0, h).wait_send()

    @pl.when(visit1 & has_prev2)
    def _():
        b_hop(1).wait_send()
        for h in range(HEADS):
            q_hop(1, h).wait_send()

    for s, given in ((0, visit1), (1, visit2)):

        @pl.when(given)
        def _():
            for h in range(HEADS):
                o_hop(s, h).wait_send()
                s_hop(s, h).wait_send()


def solution(mesh):
    n_ctx = mesh.shape["ctx"]

    def body(queries, keys, values, directions, rates, selected, out_weight):
        tokens, width = queries.shape
        shard = (tokens, width)
        dma = pltpu.SemaphoreType.DMA
        vmem = pl.BlockSpec(memory_space=pltpu.VMEM)
        slab = pltpu.VMEM(shard, bf16)
        square = pltpu.VMEM((HD, width), f32)
        state = pltpu.VMEM((3 * HEADS, tokens, HD), f32)

        def pair(shape, dtype):
            return pltpu.VMEM((2,) + shape, dtype)

        scratch = [slab] * 4 + [pltpu.VMEM(rates.shape, f32)]
        scratch += [slab] * 6 + [pair(shard, bf16), slab, square, square]
        scratch += [slab, slab, pair(shard, bf16), pair(shard, bf16)]
        scratch += [pltpu.VMEM((20, HD), f32), pair((20, HD), f32)]
        scratch += [pair(shard, bf16), pair(shard, bf16)]
        scratch += [pair((HEADS, 2, HD), f32), pair((HEADS, 2, HD), f32)]
        scratch += [state, state, state, pltpu.VMEM((HEADS, tokens, tokens), f32)]
        scratch += [pltpu.VMEM((4,) + shard, bf16), pltpu.VMEM((4, width, width), bf16)]
        each, two = (HEADS,), (2, HEADS)
        sems = [each] * 12 + [(), (), two, two, (2,), (2,), two, two, two, two]
        sems += [(3,), (3,), (3,), (3,), two, two, two, two, (), (5,)]
        scratch += [dma(s) if s else dma for s in sems]
        return pl.pallas_call(
            functools.partial(kernel, n_ctx),
            out_shape=pltpu.VMEM(shard, bf16),
            in_specs=[
                pl.BlockSpec(memory_space=pltpu.SMEM),
            ]
            + [pl.BlockSpec(memory_space=pl.ANY)] * 6,
            out_specs=vmem,
            scratch_shapes=scratch,
            compiler_params=pltpu.CompilerParams(
                collective_id=0, has_side_effects=True, vmem_limit_bytes=56 << 20
            ),
            name="path_attention",
        )(selected, queries, keys, values, directions, rates, out_weight)

    in_specs = (
        P("ctx", "head"),
        P("ctx", "head"),
        P("ctx", "head"),
        P("ctx", "head"),
        P("head", "ctx"),
        P("ctx", None),
        P("head", None),
    )
    return jax.shard_map(
        body, mesh=mesh, in_specs=in_specs, out_specs=P("ctx", "head"), check_vma=False
    )
```

```python
import functools

import jax
import jax.numpy as jnp
from jax import lax
from jax.experimental import pallas as pl
from jax.experimental.pallas import tpu as pltpu
from jax.sharding import PartitionSpec as P

MESH = pl.DeviceIdType.MESH
HD = 128
B = 128
HEADS = 4
NEG = -1e30
PAUSE_AT = 4
SCALE = HD ** (-0.5)
f32 = jnp.float32
bf16 = jnp.bfloat16
NN = (((1,), (0,)), ((), ()))
NT = (((1,), (1,)), ((), ()))
TN = (((0,), (0,)), ((), ()))


def dot(a, b, dims):
    return lax.dot_general(a, b, dims, preferred_element_type=f32)


def split(a):
    high = a.astype(bf16)
    return high, (a - high.astype(f32)).astype(bf16)


def dot3(a, b, dims):
    return dot(a[0], b[0], dims) + (dot(a[1], b[0], dims) + dot(a[0], b[1], dims))


def dot_left(a, b, dims):
    return dot(a[0], b, dims) + dot(a[1], b, dims)


def dot_right(a, b, dims):
    return dot(a, b[0], dims) + dot(a, b[1], dims)


def block_terms(q, k, w, beta, pause, pause_at):
    each = range(len(q))
    row = lax.broadcasted_iota(jnp.int32, (B, B), 0)
    col = lax.broadcasted_iota(jnp.int32, (B, B), 1)
    eye = (row == col).astype(f32)
    grams = [
        dot(jnp.concatenate([w[i], q[i]], 0), jnp.concatenate([w[i], k[i]], 0), NT) for i in each
    ]
    wide = [w[i].astype(f32) for i in each]
    norm = [jnp.sum(wide[i] * wide[i], -1, keepdims=True) for i in each]
    rate = [
        jnp.transpose(jnp.broadcast_to(beta[i], (B, B))) / (norm[i] + 1e-6) for i in each
    ]
    lower = [jnp.where(row > col, rate[i] * grams[i][:B, :B], 0.0) for i in each]
    key_proj = [split(jnp.where(row > col, grams[i][:B, B:], 0.0)) for i in each]
    query_proj = [split(jnp.where(row >= col, grams[i][B:, :B], 0.0)) for i in each]

    def off_diagonal(size):
        return ((row ^ col) < 2 * size) & ((row & size) != 0) & ((col & size) == 0)

    inverse = [eye - jnp.where(off_diagonal(1), lower[i], 0.0) for i in each]
    size = 2
    while size < B:
        mask = off_diagonal(size)
        parts = [split(inverse[i]) for i in each]
        below = [split(jnp.where(mask, lower[i], 0.0)) for i in each]
        step = [split(dot3(below[i], parts[i], NN)) for i in each]
        inverse = [inverse[i] - dot3(parts[i], step[i], NN) for i in each]
        if size == pause_at:
            pause()
        size *= 2
    mixing = [split(inverse[i] * jnp.transpose(rate[i])) for i in each]
    mix_w = [split(dot_left(mixing[i], w[i], NN)) for i in each]
    mix_k = [split(dot3(mixing[i], key_proj[i], NN)) for i in each]
    block_map = [eye - dot_right(w[i], mix_w[i], TN) for i in each]
    k_end = [k[i].astype(f32) - dot_left(mix_k[i], w[i], TN) for i in each]
    q_start = [q[i].astype(f32) - dot3(query_proj[i], mix_w[i], NN) for i in each]
    inner = [grams[i][B:, B:] - dot3(query_proj[i], mix_k[i], NN) for i in each]
    return q_start, k_end, inner, block_map


def kernel(
    n_ctx, sel_hbm, q_hbm, k_hbm, v_hbm, w_hbm, rate_hbm, ow_ref, out_ref,
    sel, q_ref, k_ref, v_ref, w_ref, rate_ref,
    k_own, k_par, k_ext, v_own, v_par, v_ext, k_stage, k_tail, d_mine, d_part,
    q_front, q_home, q_in, q_vis, b_mine, b_in, o_out, o_in, s_out, s_in,
    m_ref, l_ref, acc_ref, local, att, wfull,
    sv, rv, svp, rvp, sve, rve, sk, rk, skp, rkp, ske, rke, sd, rd, sq, rq, sb, rb, so, ro, ss, rs,
    sw, rw, swp, rwp, sa, ra, sar, rar, lw, li,
):
    me = lax.axis_index("ctx")
    x = lax.axis_index("head")
    core = lax.rem(me, 2)
    is0 = core == 0
    is1 = core == 1
    n_x = 4
    nxt = lax.rem(me + 2, n_ctx)
    prv = lax.rem(me + n_ctx - 2, n_ctx)
    partner = me + 1 - 2 * core
    cross = jnp.where(is0, lax.rem(me + n_ctx - 1, n_ctx), lax.rem(me + 1, n_ctx))
    x_right = lax.rem(x + 1, n_x)
    x_left = lax.rem(x + n_x - 1, n_x)
    x_far = lax.rem(x + 2, n_x)
    has_next = me + 2 < n_ctx
    has_next2 = me + 4 < n_ctx
    has_prev = me >= 2
    has_prev2 = me >= 4
    crossed = (is0 & has_prev) | (is1 & has_next)
    feeds = is1 & has_prev & (me + 6 < n_ctx)
    visit1 = has_prev & has_next
    visit2 = has_prev & has_next2
    lanes = [slice(h * HD, (h + 1) * HD) for h in range(HEADS)]
    rows = [slice(n * B, (n + 1) * B) for n in range(2)]

    def remote(src, dst, send, recv, to):
        return pltpu.make_async_remote_copy(
            src_ref=src, dst_ref=dst, send_sem=send, recv_sem=recv, device_id=to, device_id_type=MESH
        )

    barrier = pltpu.get_barrier_semaphore()
    for other, there in ((nxt, has_next), (prv, has_prev), (cross, crossed)):

        @pl.when(there)
        def _():
            pl.semaphore_signal(barrier, inc=1, device_id=(other, x), device_id_type=MESH)

    pl.semaphore_signal(barrier, inc=1, device_id=(partner, x), device_id_type=MESH)
    for other in (x_right, x_far, x_left):
        pl.semaphore_signal(barrier, inc=1, device_id=(me, other), device_id_type=MESH)
    count = lambda flag: jnp.where(flag, 1, 0)
    greetings = 4 + count(has_next) + count(has_prev) + count(crossed)
    inputs = [
        pltpu.make_async_copy(source, target, li.at[i])
        for i, (source, target) in enumerate(
            (
                (sel_hbm, sel), (w_hbm, w_ref), (k_hbm, k_ref), (q_hbm, q_ref),
                (rate_hbm, rate_ref), (v_hbm, v_ref),
            )
        )
    ]
    for copy in inputs:
        copy.start()

    def v_hop(h):
        return remote(v_hbm.at[:, lanes[h]], v_own.at[:, lanes[h]], sv.at[h], rv.at[h], (nxt, x))

    def k_hop(h):
        return remote(
            k_stage.at[0, :, lanes[h]], k_own.at[:, lanes[h]], sk.at[h], rk.at[h], (nxt, x)
        )

    def v_share(h):
        return remote(
            v_own.at[:, lanes[h]], v_par.at[:, lanes[h]], svp.at[h], rvp.at[h], (partner, x)
        )

    def k_share(h):
        return remote(
            k_own.at[:, lanes[h]], k_par.at[:, lanes[h]], skp.at[h], rkp.at[h], (partner, x)
        )

    def v_extra(h, src, to):
        return remote(src.at[:, lanes[h]], v_ext.at[:, lanes[h]], sve.at[h], rve.at[h], (to, x))

    def k_extra(h, src, to):
        return remote(src.at[:, lanes[h]], k_ext.at[:, lanes[h]], ske.at[h], rke.at[h], (to, x))

    def q_hop(s, h):
        src = q_home.at[:, lanes[h]] if s == 0 else q_vis.at[0, :, lanes[h]]
        return remote(src, q_in.at[s, :, lanes[h]], sq.at[s, h], rq.at[s, h], (prv, x))

    def b_hop(s):
        src = b_mine if s == 0 else b_in.at[0]
        return remote(src, b_in.at[s], sb.at[s], rb.at[s], (prv, x))

    def o_hop(s, h):
        return remote(
            o_out.at[s, :, lanes[h]], o_in.at[s, :, lanes[h]], so.at[s, h], ro.at[s, h], (nxt, x)
        )

    def s_hop(s, h):
        return remote(s_out.at[s, h], s_in.at[s, h], ss.at[s, h], rs.at[s, h], (nxt, x))

    half = pl.ds(pl.multiple_of(core * 256, 256), 256)
    other_half = pl.ds(pl.multiple_of((1 - core) * 256, 256), 256)
    peers = [(x_right, x_left), (x_far, x_far), (x_left, x_right)]

    def w_send(r):
        to = peers[r][0]
        cols = pl.ds(pl.multiple_of(to * 512, 512), 512)
        return remote(ow_ref.at[half, cols], wfull.at[x, half], sw.at[r], rw.at[r], (me, to))

    def w_recv(r):
        src = peers[r][1]
        return remote(wfull.at[src, half], wfull.at[src, half], sw.at[r], rw.at[r], (me, src))

    def w_share(r, part):
        slot = wfull.at[peers[r][1], part]
        return remote(slot, slot, swp.at[r], rwp.at[r], (partner, x))

    def a_hop(r, h, part, owner, to):
        slot = att.at[owner, rows[part], lanes[h]]
        return remote(slot, slot, sa.at[r, h, part], ra.at[r, h, part], (me, to))

    def a_relay(r, h, owner, to):
        slot = att.at[owner, rows[r], lanes[h]]
        return remote(slot, slot, sar.at[r, h], rar.at[r, h], (me, to))

    own_w = pltpu.make_async_copy(
        ow_ref.at[:, pl.ds(pl.multiple_of(x * 512, 512), 512)], wfull.at[x], lw
    )

    def leave():
        pl.semaphore_wait(barrier, greetings)

        @pl.when(has_next)
        def _():
            for h in range(HEADS):
                v_hop(h).start()

        @pl.when(is0)
        def _():
            for h in range(HEADS):
                v_extra(h, v_hbm, partner).start()

        for r in range(3):
            w_send(r).start()
        own_w.start()

        @pl.when(has_prev2)
        def _():
            b_hop(0).start()

    def bias(n, block):
        hit = sel[n, 0] == block
        for e in range(1, 4):
            hit = hit | (sel[n, e] == block)
        return jnp.where(hit, 0.0, NEG).astype(f32)

    inputs[0].wait()
    away = [me - 4, me - 3 - 2 * core, me - 6, me - 5 - 2 * core, jnp.where(is0, me - 7, -1)]
    for n in range(2):
        for i, device in enumerate(away):
            for b in range(2):
                line = 10 * n + 2 * i + b
                b_mine[line : line + 1, :] = jnp.full((1, HD), bias(n, 2 * device + b), f32)

    @pl.when(is0 & (me < 4))
    def _():
        k_ext[...] = jnp.zeros_like(k_ext)
        v_ext[...] = jnp.zeros_like(v_ext)

    pairs = [(n, h) for h in range(HEADS) for n in range(2)]

    def cut(ref):
        return [ref[rows[n], lanes[h]] for n, h in pairs]

    for copy in inputs[1:5]:
        copy.wait()
    q_start, k_end, inner, block_map = block_terms(
        cut(q_ref), cut(k_ref), cut(w_ref), [rate_ref[h : h + 1, rows[n]] for n, h in pairs],
        leave, PAUSE_AT,
    )
    maps = [split(m) for m in block_map]
    tails, fronts = [], []
    for h in range(HEADS):
        d_mine[:, lanes[h]] = dot3(maps[2 * h + 1], maps[2 * h], NN)
    exchange_d = remote(d_mine, d_part, sd, rd, (partner, x))
    exchange_d.start()
    for h in range(HEADS):
        first, second = 2 * h, 2 * h + 1
        early = split(k_end[first])
        tails.append(jnp.concatenate([dot3(early, maps[second], NT), k_end[second]], 0))
        late = split(q_start[second])
        fronts.append(jnp.concatenate([q_start[first], dot3(late, maps[first], NN)], 0))
        q_front[:, lanes[h]] = (fronts[h] * SCALE).astype(bf16)
        k_tail[:, lanes[h]] = tails[h].astype(bf16)
        local[h, B:, :B] = dot3(late, early, NT) * SCALE
        local[h, :B, :B] = inner[first] * SCALE
        local[h, B:, B:] = inner[second] * SCALE

    @pl.when(is0)
    def _():
        for h in range(HEADS):
            k_extra(h, k_tail, partner).start()

    def pass_values(heads):
        @pl.when(has_prev)
        def _():
            for h in heads:
                v_hop(h).wait_recv()
                v_share(h).start()

    pass_values((0,))
    exchange_d.wait_recv()
    others = [split(d_part[:, lanes[h]]) for h in range(HEADS)]
    for h in range(HEADS):
        moved = dot3(split(fronts[h]), others[h], NN)
        q_home[:, lanes[h]] = (jnp.where(is0, fronts[h], moved) * SCALE).astype(bf16)

    @pl.when(has_prev2)
    def _():
        for h in range(HEADS):
            q_hop(0, h).start()

    for h in range(HEADS):
        carried = dot3(split(tails[h]), others[h], NT)
        k_stage[0, :, lanes[h]] = jnp.where(is0, carried, tails[h]).astype(bf16)

    @pl.when(has_next)
    def _():
        for h in range(HEADS):
            k_hop(h).start()

    chip_maps = []
    for h in range(HEADS):
        d_own = d_mine[:, lanes[h]]
        d_other = d_part[:, lanes[h]]
        later = jnp.where(is0, d_other, d_own)
        sooner = jnp.where(is0, d_own, d_other)
        chip_maps.append(split(dot3(split(later), split(sooner), NN)))
    pass_values((1, 2, 3))

    def first_block(h):
        row = lax.broadcasted_iota(jnp.int32, (B, B), 0)
        col = lax.broadcasted_iota(jnp.int32, (B, B), 1)
        for n in range(2):
            tiles = [local[h, rows[n], rows[b]] + bias(n, 2 * me + b) for b in range(n)]
            tiles.append(
                jnp.where(row >= col, local[h, rows[n], rows[n]] + bias(n, 2 * me + n), NEG)
            )
            top = functools.reduce(jnp.maximum, tiles)
            top = jnp.broadcast_to(jnp.max(top, -1, keepdims=True), (B, B))
            expos = [jnp.exp(t - top) for t in tiles]
            m_ref[h, rows[n], :] = top
            l_ref[h, rows[n], :] = functools.reduce(jnp.add, expos)
            total = jnp.zeros((B, HD), f32)
            for b, e in enumerate(expos):
                total = total + dot(e.astype(bf16), v_ref[rows[b], lanes[h]], NN)
            acc_ref[h, rows[n], :] = total

    def attend(g, query, sources, fresh=False):
        scores = [dot(query, keys, NT) for keys, _, _ in sources]
        for n in range(2):
            tiles = [
                scores[i][rows[n], rows[b]] + offset(n, b)
                for i, (_, _, offset) in enumerate(sources)
                for b in range(2)
            ]
            top = functools.reduce(jnp.maximum, tiles)
            top = jnp.broadcast_to(jnp.max(top, -1, keepdims=True), (B, B))
            if not fresh:
                old = m_ref[g, rows[n], :]
                top = jnp.maximum(old, top)
                fade = jnp.exp(old - top)
            expos = [jnp.exp(t - top) for t in tiles]
            norm = functools.reduce(jnp.add, expos)
            if not fresh:
                norm = norm + l_ref[g, rows[n], :] * fade
            m_ref[g, rows[n], :] = top
            l_ref[g, rows[n], :] = norm
            total = None if fresh else acc_ref[g, rows[n], :] * fade
            for i, (_, values, _) in enumerate(sources):
                weights = jnp.concatenate(expos[2 * i : 2 * i + 2], 1).astype(bf16)
                part = dot(weights, values, NN)
                total = part if total is None else total + part
            acc_ref[g, rows[n], :] = total

    def at_home(device):
        return lambda n, b: bias(n, 2 * device + b)

    def sent_along(s, i):
        def offset(n, b):
            line = 10 * n + 2 * i + b
            return b_in[s, line : line + 1, :]

        return offset

    def shards(h, own, other):
        return [
            (k_own[:, lanes[h]], v_own[:, lanes[h]], own),
            (k_par[:, lanes[h]], v_par[:, lanes[h]], other),
        ]

    def wait_extra(h):
        v_extra(h, v_own, cross).wait_recv()
        k_extra(h, k_tail, cross).wait_recv()

    def result(g):
        parts, logs = [], []
        for n in range(2):
            norm = jnp.sum(l_ref[g, rows[n], :], -1, keepdims=True)
            parts.append(acc_ref[g, rows[n], :] / norm)
            logs.append(jnp.transpose(m_ref[g, rows[n], :] + jnp.log(norm))[:1, :])
        return parts, logs

    def give(s, h):
        parts, logs = result((s + 1) * HEADS + h)
        for n in range(2):
            o_out[s, rows[n], lanes[h]] = parts[n].astype(bf16)
            s_out[s, h, n : n + 1, :] = logs[n]
        o_hop(s, h).start()
        s_hop(s, h).start()

    def take(s, h):
        o_hop(s, h).wait_recv()
        s_hop(s, h).wait_recv()
        g = s * HEADS + h
        for n in range(2):
            log = jnp.transpose(jnp.broadcast_to(s_in[s, h, n : n + 1, :], (B, B)))
            old = m_ref[g, rows[n], :]
            top = jnp.maximum(old, log)
            fade, weight = jnp.exp(old - top), jnp.exp(log - top)
            m_ref[g, rows[n], :] = top
            l_ref[g, rows[n], :] = l_ref[g, rows[n], :] * fade + weight * (1.0 / B)
            acc_ref[g, rows[n], :] = (
                acc_ref[g, rows[n], :] * fade + o_in[s, rows[n], lanes[h]].astype(f32) * weight
            )

    inputs[5].wait()
    for h in range(HEADS):
        first_block(h)

    @pl.when(is1)
    def _():
        for h in range(HEADS):
            wait_extra(h)
            attend(h, q_front[:, lanes[h]], [(k_ext[:, lanes[h]], v_ext[:, lanes[h]], at_home(me - 1))])

    @pl.when(visit1)
    def _():
        b_hop(0).wait_recv()

        @pl.when(has_prev2)
        def _():
            b_hop(1).start()

    def wait_share(h):
        v_share(h).wait_recv()
        k_share(h).wait_recv()

    def near(h):
        device = me - 2
        attend(
            h,
            q_home[:, lanes[h]],
            shards(h, at_home(device), at_home(device + 1 - 2 * core)),
        )
        attend(
            HEADS + h,
            q_vis[0, :, lanes[h]],
            shards(h, sent_along(0, 0), sent_along(0, 1)),
            fresh=True,
        )

    @pl.when(has_prev)
    def _():
        for h in range(HEADS):
            k_hop(h).wait_recv()
            k_share(h).start()

            @pl.when(feeds)
            def _():
                moved = dot_right(k_own[:, lanes[h]], chip_maps[h], NT)
                k_stage[1, :, lanes[h]] = moved.astype(bf16)
                k_extra(h, k_stage.at[1], cross).start()
                v_extra(h, v_own, cross).start()

            @pl.when(visit1)
            def _():
                q_hop(0, h).wait_recv()
                moved = dot_right(q_in[0, :, lanes[h]], chip_maps[h], NN)
                q_vis[0, :, lanes[h]] = moved.astype(bf16)

                @pl.when(has_prev2)
                def _():
                    q_hop(1, h).start()

            if h > 0:
                wait_share(h - 1)
                near(h - 1)
        wait_share(HEADS - 1)

    def far(h):
        @pl.when(visit2)
        def _():
            q_hop(1, h).wait_recv()
            moved = dot_right(q_in[1, :, lanes[h]], chip_maps[h], NN)
            q_vis[1, :, lanes[h]] = moved.astype(bf16)

            @pl.when(is0 & has_prev2)
            def _():
                wait_extra(h)

            attend(
                2 * HEADS + h,
                q_vis[1, :, lanes[h]],
                shards(h, sent_along(1, 2), sent_along(1, 3))
                + [(k_ext[:, lanes[h]], v_ext[:, lanes[h]], sent_along(1, 4))],
                fresh=True,
            )
            give(1, h)

    def back(h):
        @pl.when(visit1)
        def _():
            @pl.when(has_prev2)
            def _():
                take(1, h)

            give(0, h)

    @pl.when(visit2)
    def _():
        b_hop(1).wait_recv()

    far(0)
    far(1)
    far(2)

    @pl.when(has_prev)
    def _():
        near(HEADS - 1)

    for r in range(3):
        w_recv(r).wait_recv()
        w_share(r, half).start()
    back(0)
    far(3)
    back(1)
    back(2)

    def pass_head(h):
        a_hop(0, h, 0, x_left, x_left).wait_recv()
        a_relay(0, h, x_left, x_right).start()
        a_hop(1, h, 1, x_right, x_right).wait_recv()
        a_relay(1, h, x_right, x_left).start()

    def finish(h):
        @pl.when(has_prev2)
        def _():
            take(0, h)

        parts, _ = result(h)
        for n in range(2):
            att[x, rows[n], lanes[h]] = parts[n].astype(bf16)
        for part in range(2):
            a_hop(0, h, part, x, x_right).start()
            a_hop(1, h, 1 - part, x, x_left).start()

    finish(0)
    back(3)
    finish(1)
    finish(2)
    pass_head(0)
    finish(3)
    pass_head(1)

    for r in range(3):
        w_share(r, other_half).wait_recv()
    own_w.wait()
    total = dot(att[x], wfull[x], NN)

    def near_part(total, h):
        a_hop(0, h, 1, x_left, x_left).wait_recv()
        a_hop(1, h, 0, x_right, x_right).wait_recv()
        for src in (x_left, x_right):
            total = total + dot(att[src, :, lanes[h]], wfull[src, lanes[h], :], NN)
        return total

    pass_head(2)
    pass_head(3)
    total = near_part(near_part(total, 0), 1)
    total = near_part(near_part(total, 2), 3)
    for h in range(HEADS):
        a_relay(0, h, x_far, x_left).wait_recv()
        a_relay(1, h, x_far, x_right).wait_recv()
        total = total + dot(att[x_far, :, lanes[h]], wfull[x_far, lanes[h], :], NN)
    out_ref[...] = total.astype(bf16)

    exchange_d.wait_send()
    for r in range(3):
        w_send(r).wait_send()
        w_share(r, half).wait_send()
    for h in range(HEADS):
        for part in range(2):
            a_hop(0, h, part, x, x_right).wait_send()
            a_hop(1, h, part, x, x_left).wait_send()
        a_relay(0, h, x_left, x_right).wait_send()
        a_relay(1, h, x_right, x_left).wait_send()

    @pl.when(has_next)
    def _():
        for h in range(HEADS):
            v_hop(h).wait_send()
            k_hop(h).wait_send()

    @pl.when(has_prev)
    def _():
        for h in range(HEADS):
            v_share(h).wait_send()
            k_share(h).wait_send()

    @pl.when(is0 | feeds)
    def _():
        for h in range(HEADS):
            v_extra(h, v_own, cross).wait_send()
            k_extra(h, k_tail, cross).wait_send()

    @pl.when(has_prev2)
    def _():
        b_hop(0).wait_send()
        for h in range(HEADS):
            q_hop(0, h).wait_send()

    @pl.when(visit1 & has_prev2)
    def _():
        b_hop(1).wait_send()
        for h in range(HEADS):
            q_hop(1, h).wait_send()

    for s, given in ((0, visit1), (1, visit2)):

        @pl.when(given)
        def _():
            for h in range(HEADS):
                o_hop(s, h).wait_send()
                s_hop(s, h).wait_send()


def solution(mesh):
    n_ctx = mesh.shape["ctx"]

    def body(queries, keys, values, directions, rates, selected, out_weight):
        tokens, width = queries.shape
        shard = (tokens, width)
        dma = pltpu.SemaphoreType.DMA
        vmem = pl.BlockSpec(memory_space=pltpu.VMEM)
        slab = pltpu.VMEM(shard, bf16)
        square = pltpu.VMEM((HD, width), f32)
        state = pltpu.VMEM((3 * HEADS, tokens, HD), f32)

        def pair(shape, dtype):
            return pltpu.VMEM((2,) + shape, dtype)

        scratch = [pltpu.SMEM(selected.shape, jnp.int32)] + [slab] * 4 + [pltpu.VMEM(rates.shape, f32)]
        scratch += [slab] * 6 + [pair(shard, bf16), slab, square, square]
        scratch += [slab, slab, pair(shard, bf16), pair(shard, bf16)]
        scratch += [pltpu.VMEM((20, HD), f32), pair((20, HD), f32)]
        scratch += [pair(shard, bf16), pair(shard, bf16)]
        scratch += [pair((HEADS, 2, HD), f32), pair((HEADS, 2, HD), f32)]
        scratch += [state, state, state, pltpu.VMEM((HEADS, tokens, tokens), f32)]
        scratch += [pltpu.VMEM((4,) + shard, bf16), pltpu.VMEM((4, width, width), bf16)]
        each, two, halves = (HEADS,), (2, HEADS), (2, HEADS, 2)
        sems = [each] * 12 + [(), (), two, two, (2,), (2,), two, two, two, two]
        sems += [(3,), (3,), (3,), (3,), halves, halves, two, two, (), (6,)]
        scratch += [dma(s) if s else dma for s in sems]
        return pl.pallas_call(
            functools.partial(kernel, n_ctx),
            out_shape=pltpu.VMEM(shard, bf16),
            in_specs=[
            ]
            + [pl.BlockSpec(memory_space=pl.ANY)] * 7,
            out_specs=vmem,
            scratch_shapes=scratch,
            compiler_params=pltpu.CompilerParams(
                collective_id=0, has_side_effects=True, vmem_limit_bytes=56 << 20
            ),
            name="path_attention",
        )(selected, queries, keys, values, directions, rates, out_weight)

    in_specs = (
        P("ctx", "head"),
        P("ctx", "head"),
        P("ctx", "head"),
        P("ctx", "head"),
        P("head", "ctx"),
        P("ctx", None),
        P("head", None),
    )
    return jax.shard_map(
        body, mesh=mesh, in_specs=in_specs, out_specs=P("ctx", "head"), check_vma=False
    )
```

```python
import functools

import jax
import jax.numpy as jnp
from jax import lax
from jax.experimental import pallas as pl
from jax.experimental.pallas import tpu as pltpu
from jax.sharding import PartitionSpec as P

MESH = pl.DeviceIdType.MESH
HD = 128
B = 128
HEADS = 4
NEG = -1e30
PAUSE_AT = 4
SCALE = HD ** (-0.5)
f32 = jnp.float32
bf16 = jnp.bfloat16
NN = (((1,), (0,)), ((), ()))
NT = (((1,), (1,)), ((), ()))
TN = (((0,), (0,)), ((), ()))


def dot(a, b, dims):
    return lax.dot_general(a, b, dims, preferred_element_type=f32)


def split(a):
    high = a.astype(bf16)
    return high, (a - high.astype(f32)).astype(bf16)


def dot3(a, b, dims):
    return dot(a[0], b[0], dims) + (dot(a[1], b[0], dims) + dot(a[0], b[1], dims))


def dot_left(a, b, dims):
    return dot(a[0], b, dims) + dot(a[1], b, dims)


def dot_right(a, b, dims):
    return dot(a, b[0], dims) + dot(a, b[1], dims)


def block_terms(q, k, w, beta, pause, pause_at):
    each = range(len(q))
    row = lax.broadcasted_iota(jnp.int32, (B, B), 0)
    col = lax.broadcasted_iota(jnp.int32, (B, B), 1)
    eye = (row == col).astype(f32)
    grams = [
        dot(jnp.concatenate([w[i], q[i]], 0), jnp.concatenate([w[i], k[i]], 0), NT) for i in each
    ]
    wide = [w[i].astype(f32) for i in each]
    norm = [jnp.sum(wide[i] * wide[i], -1, keepdims=True) for i in each]
    rate = [
        jnp.transpose(jnp.broadcast_to(beta[i], (B, B))) / (norm[i] + 1e-6) for i in each
    ]
    lower = [jnp.where(row > col, rate[i] * grams[i][:B, :B], 0.0) for i in each]
    key_proj = [split(jnp.where(row > col, grams[i][:B, B:], 0.0)) for i in each]
    query_proj = [split(jnp.where(row >= col, grams[i][B:, :B], 0.0)) for i in each]

    def off_diagonal(size):
        return ((row ^ col) < 2 * size) & ((row & size) != 0) & ((col & size) == 0)

    inverse = [eye - jnp.where(off_diagonal(1), lower[i], 0.0) for i in each]
    size = 2
    while size < B:
        mask = off_diagonal(size)
        parts = [split(inverse[i]) for i in each]
        below = [split(jnp.where(mask, lower[i], 0.0)) for i in each]
        step = [split(dot3(below[i], parts[i], NN)) for i in each]
        inverse = [inverse[i] - dot3(parts[i], step[i], NN) for i in each]
        if size == pause_at:
            pause()
        size *= 2
    mixing = [split(inverse[i] * jnp.transpose(rate[i])) for i in each]
    mix_w = [split(dot_left(mixing[i], w[i], NN)) for i in each]
    mix_k = [split(dot3(mixing[i], key_proj[i], NN)) for i in each]
    block_map = [eye - dot_right(w[i], mix_w[i], TN) for i in each]
    k_end = [k[i].astype(f32) - dot_left(mix_k[i], w[i], TN) for i in each]
    q_start = [q[i].astype(f32) - dot3(query_proj[i], mix_w[i], NN) for i in each]
    inner = [grams[i][B:, B:] - dot3(query_proj[i], mix_k[i], NN) for i in each]
    return q_start, k_end, inner, block_map


def kernel(
    n_ctx, sel_hbm, q_hbm, k_hbm, v_hbm, w_hbm, rate_hbm, ow_ref, out_ref,
    sel, q_ref, k_ref, v_ref, w_ref, rate_ref,
    k_own, k_par, k_ext, v_own, v_par, v_ext, k_stage, k_tail, d_mine, d_part,
    q_front, q_home, q_in, q_vis, b_mine, b_in, o_out, o_in, s_out, s_in,
    m_ref, l_ref, acc_ref, local, att, wfull,
    sv, rv, svp, rvp, sve, rve, sk, rk, skp, rkp, ske, rke, sd, rd, sq, rq, sb, rb, so, ro, ss, rs,
    sw, rw, swp, rwp, sa, ra, sar, rar, lw, li,
):
    me = lax.axis_index("ctx")
    x = lax.axis_index("head")
    core = lax.rem(me, 2)
    is0 = core == 0
    is1 = core == 1
    n_x = 4
    nxt = lax.rem(me + 2, n_ctx)
    prv = lax.rem(me + n_ctx - 2, n_ctx)
    partner = me + 1 - 2 * core
    cross = jnp.where(is0, lax.rem(me + n_ctx - 1, n_ctx), lax.rem(me + 1, n_ctx))
    x_right = lax.rem(x + 1, n_x)
    x_left = lax.rem(x + n_x - 1, n_x)
    x_far = lax.rem(x + 2, n_x)
    has_next = me + 2 < n_ctx
    has_next2 = me + 4 < n_ctx
    has_prev = me >= 2
    has_prev2 = me >= 4
    crossed = (is0 & has_prev) | (is1 & has_next)
    feeds = is1 & has_prev & (me + 6 < n_ctx)
    visit1 = has_prev & has_next
    visit2 = has_prev & has_next2
    lanes = [slice(h * HD, (h + 1) * HD) for h in range(HEADS)]
    rows = [slice(n * B, (n + 1) * B) for n in range(2)]

    def remote(src, dst, send, recv, to):
        return pltpu.make_async_remote_copy(
            src_ref=src, dst_ref=dst, send_sem=send, recv_sem=recv, device_id=to, device_id_type=MESH
        )

    barrier = pltpu.get_barrier_semaphore()
    for other, there in ((nxt, has_next), (prv, has_prev), (cross, crossed)):

        @pl.when(there)
        def _():
            pl.semaphore_signal(barrier, inc=1, device_id=(other, x), device_id_type=MESH)

    pl.semaphore_signal(barrier, inc=1, device_id=(partner, x), device_id_type=MESH)
    for other in (x_right, x_far, x_left):
        pl.semaphore_signal(barrier, inc=1, device_id=(me, other), device_id_type=MESH)
    count = lambda flag: jnp.where(flag, 1, 0)
    greetings = 4 + count(has_next) + count(has_prev) + count(crossed)
    inputs = [
        pltpu.make_async_copy(source, target, li.at[i])
        for i, (source, target) in enumerate(
            (
                (sel_hbm, sel), (w_hbm, w_ref), (k_hbm, k_ref), (q_hbm, q_ref),
                (rate_hbm, rate_ref), (v_hbm, v_ref),
            )
        )
    ]
    for copy in inputs:
        copy.start()

    def v_hop(h):
        return remote(v_hbm.at[:, lanes[h]], v_own.at[:, lanes[h]], sv.at[h], rv.at[h], (nxt, x))

    def k_hop(h):
        return remote(
            k_stage.at[0, :, lanes[h]], k_own.at[:, lanes[h]], sk.at[h], rk.at[h], (nxt, x)
        )

    def v_share(h):
        return remote(
            v_own.at[:, lanes[h]], v_par.at[:, lanes[h]], svp.at[h], rvp.at[h], (partner, x)
        )

    def k_share(h):
        return remote(
            k_own.at[:, lanes[h]], k_par.at[:, lanes[h]], skp.at[h], rkp.at[h], (partner, x)
        )

    def v_extra(h, src, to):
        return remote(src.at[:, lanes[h]], v_ext.at[:, lanes[h]], sve.at[h], rve.at[h], (to, x))

    def k_extra(h, src, to):
        return remote(src.at[:, lanes[h]], k_ext.at[:, lanes[h]], ske.at[h], rke.at[h], (to, x))

    def q_hop(s, h):
        src = q_home.at[:, lanes[h]] if s == 0 else q_vis.at[0, :, lanes[h]]
        return remote(src, q_in.at[s, :, lanes[h]], sq.at[s, h], rq.at[s, h], (prv, x))

    def b_hop(s):
        src = b_mine if s == 0 else b_in.at[0]
        return remote(src, b_in.at[s], sb.at[s], rb.at[s], (prv, x))

    def o_hop(s, h, n):
        return remote(
            o_out.at[s, rows[n], lanes[h]], o_in.at[s, rows[n], lanes[h]],
            so.at[s, h, n], ro.at[s, h, n], (nxt, x),
        )

    def s_hop(s, h):
        return remote(s_out.at[s, h], s_in.at[s, h], ss.at[s, h], rs.at[s, h], (nxt, x))

    half = pl.ds(pl.multiple_of(core * 256, 256), 256)
    other_half = pl.ds(pl.multiple_of((1 - core) * 256, 256), 256)
    peers = [(x_right, x_left), (x_far, x_far), (x_left, x_right)]

    def w_send(r):
        to = peers[r][0]
        cols = pl.ds(pl.multiple_of(to * 512, 512), 512)
        return remote(ow_ref.at[half, cols], wfull.at[x, half], sw.at[r], rw.at[r], (me, to))

    def w_recv(r):
        src = peers[r][1]
        return remote(wfull.at[src, half], wfull.at[src, half], sw.at[r], rw.at[r], (me, src))

    def w_share(r, part):
        slot = wfull.at[peers[r][1], part]
        return remote(slot, slot, swp.at[r], rwp.at[r], (partner, x))

    def a_hop(r, h, part, owner, to):
        slot = att.at[owner, rows[part], lanes[h]]
        return remote(slot, slot, sa.at[r, h, part], ra.at[r, h, part], (me, to))

    def a_relay(r, h, owner, to):
        slot = att.at[owner, rows[r], lanes[h]]
        return remote(slot, slot, sar.at[r, h], rar.at[r, h], (me, to))

    own_w = pltpu.make_async_copy(
        ow_ref.at[:, pl.ds(pl.multiple_of(x * 512, 512), 512)], wfull.at[x], lw
    )

    def leave():
        pl.semaphore_wait(barrier, greetings)

        @pl.when(has_next)
        def _():
            for h in range(HEADS):
                v_hop(h).start()

        @pl.when(is0)
        def _():
            for h in range(HEADS):
                v_extra(h, v_hbm, partner).start()

        for r in range(3):
            w_send(r).start()
        own_w.start()

        @pl.when(has_prev2)
        def _():
            b_hop(0).start()

    def bias(n, block):
        hit = sel[n, 0] == block
        for e in range(1, 4):
            hit = hit | (sel[n, e] == block)
        return jnp.where(hit, 0.0, NEG).astype(f32)

    inputs[0].wait()
    away = [me - 4, me - 3 - 2 * core, me - 6, me - 5 - 2 * core, jnp.where(is0, me - 7, -1)]
    for n in range(2):
        for i, device in enumerate(away):
            for b in range(2):
                line = 10 * n + 2 * i + b
                b_mine[line : line + 1, :] = jnp.full((1, HD), bias(n, 2 * device + b), f32)

    @pl.when(is0 & (me < 4))
    def _():
        k_ext[...] = jnp.zeros_like(k_ext)
        v_ext[...] = jnp.zeros_like(v_ext)

    pairs = [(n, h) for h in range(HEADS) for n in range(2)]

    def cut(ref):
        return [ref[rows[n], lanes[h]] for n, h in pairs]

    for copy in inputs[1:5]:
        copy.wait()
    q_start, k_end, inner, block_map = block_terms(
        cut(q_ref), cut(k_ref), cut(w_ref), [rate_ref[h : h + 1, rows[n]] for n, h in pairs],
        leave, PAUSE_AT,
    )
    maps = [split(m) for m in block_map]
    tails, fronts = [], []
    for h in range(HEADS):
        d_mine[:, lanes[h]] = dot3(maps[2 * h + 1], maps[2 * h], NN)
    exchange_d = remote(d_mine, d_part, sd, rd, (partner, x))
    exchange_d.start()
    for h in range(HEADS):
        first, second = 2 * h, 2 * h + 1
        early = split(k_end[first])
        tails.append(jnp.concatenate([dot3(early, maps[second], NT), k_end[second]], 0))
        late = split(q_start[second])
        fronts.append(jnp.concatenate([q_start[first], dot3(late, maps[first], NN)], 0))
        q_front[:, lanes[h]] = (fronts[h] * SCALE).astype(bf16)
        k_tail[:, lanes[h]] = tails[h].astype(bf16)
        local[h, B:, :B] = dot3(late, early, NT) * SCALE
        local[h, :B, :B] = inner[first] * SCALE
        local[h, B:, B:] = inner[second] * SCALE

    @pl.when(is0)
    def _():
        for h in range(HEADS):
            k_extra(h, k_tail, partner).start()

    def pass_values(heads):
        @pl.when(has_prev)
        def _():
            for h in heads:
                v_hop(h).wait_recv()
                v_share(h).start()

    pass_values((0,))
    exchange_d.wait_recv()
    others = [split(d_part[:, lanes[h]]) for h in range(HEADS)]
    for h in range(HEADS):
        moved = dot3(split(fronts[h]), others[h], NN)
        q_home[:, lanes[h]] = (jnp.where(is0, fronts[h], moved) * SCALE).astype(bf16)

    @pl.when(has_prev2)
    def _():
        for h in range(HEADS):
            q_hop(0, h).start()

    for h in range(HEADS):
        carried = dot3(split(tails[h]), others[h], NT)
        k_stage[0, :, lanes[h]] = jnp.where(is0, carried, tails[h]).astype(bf16)

    @pl.when(has_next)
    def _():
        for h in range(HEADS):
            k_hop(h).start()

    chip_maps = []
    for h in range(HEADS):
        d_own = d_mine[:, lanes[h]]
        d_other = d_part[:, lanes[h]]
        later = jnp.where(is0, d_other, d_own)
        sooner = jnp.where(is0, d_own, d_other)
        chip_maps.append(split(dot3(split(later), split(sooner), NN)))
    pass_values((1, 2, 3))

    def first_block(h):
        row = lax.broadcasted_iota(jnp.int32, (B, B), 0)
        col = lax.broadcasted_iota(jnp.int32, (B, B), 1)
        for n in range(2):
            tiles = [local[h, rows[n], rows[b]] + bias(n, 2 * me + b) for b in range(n)]
            tiles.append(
                jnp.where(row >= col, local[h, rows[n], rows[n]] + bias(n, 2 * me + n), NEG)
            )
            top = functools.reduce(jnp.maximum, tiles)
            top = jnp.broadcast_to(jnp.max(top, -1, keepdims=True), (B, B))
            expos = [jnp.exp(t - top) for t in tiles]
            m_ref[h, rows[n], :] = top
            l_ref[h, rows[n], :] = functools.reduce(jnp.add, expos)
            total = jnp.zeros((B, HD), f32)
            for b, e in enumerate(expos):
                total = total + dot(e.astype(bf16), v_ref[rows[b], lanes[h]], NN)
            acc_ref[h, rows[n], :] = total

    def attend(g, query, sources, fresh=False):
        scores = [dot(query, keys, NT) for keys, _, _ in sources]
        for n in range(2):
            tiles = [
                scores[i][rows[n], rows[b]] + offset(n, b)
                for i, (_, _, offset) in enumerate(sources)
                for b in range(2)
            ]
            top = functools.reduce(jnp.maximum, tiles)
            top = jnp.broadcast_to(jnp.max(top, -1, keepdims=True), (B, B))
            if not fresh:
                old = m_ref[g, rows[n], :]
                top = jnp.maximum(old, top)
                fade = jnp.exp(old - top)
            expos = [jnp.exp(t - top) for t in tiles]
            norm = functools.reduce(jnp.add, expos)
            if not fresh:
                norm = norm + l_ref[g, rows[n], :] * fade
            m_ref[g, rows[n], :] = top
            l_ref[g, rows[n], :] = norm
            total = None if fresh else acc_ref[g, rows[n], :] * fade
            for i, (_, values, _) in enumerate(sources):
                weights = jnp.concatenate(expos[2 * i : 2 * i + 2], 1).astype(bf16)
                part = dot(weights, values, NN)
                total = part if total is None else total + part
            acc_ref[g, rows[n], :] = total

    def at_home(device):
        return lambda n, b: bias(n, 2 * device + b)

    def sent_along(s, i):
        def offset(n, b):
            line = 10 * n + 2 * i + b
            return b_in[s, line : line + 1, :]

        return offset

    def shards(h, own, other):
        return [
            (k_own[:, lanes[h]], v_own[:, lanes[h]], own),
            (k_par[:, lanes[h]], v_par[:, lanes[h]], other),
        ]

    def wait_extra(h):
        v_extra(h, v_own, cross).wait_recv()
        k_extra(h, k_tail, cross).wait_recv()

    def result(g):
        parts, logs = [], []
        for n in range(2):
            norm = jnp.sum(l_ref[g, rows[n], :], -1, keepdims=True)
            parts.append(acc_ref[g, rows[n], :] / norm)
            logs.append(jnp.transpose(m_ref[g, rows[n], :] + jnp.log(norm))[:1, :])
        return parts, logs

    def give(s, h):
        parts, logs = result((s + 1) * HEADS + h)
        for n in range(2):
            o_out[s, rows[n], lanes[h]] = parts[n].astype(bf16)
            s_out[s, h, n : n + 1, :] = logs[n]
        s_hop(s, h).start()
        for n in range(2):
            o_hop(s, h, n).start()

    def merge(s, h, n):
        g = s * HEADS + h
        o_hop(s, h, n).wait_recv()
        log = jnp.transpose(jnp.broadcast_to(s_in[s, h, n : n + 1, :], (B, B)))
        old = m_ref[g, rows[n], :]
        top = jnp.maximum(old, log)
        fade, weight = jnp.exp(old - top), jnp.exp(log - top)
        m_ref[g, rows[n], :] = top
        l_ref[g, rows[n], :] = l_ref[g, rows[n], :] * fade + weight * (1.0 / B)
        acc_ref[g, rows[n], :] = (
            acc_ref[g, rows[n], :] * fade + o_in[s, rows[n], lanes[h]].astype(f32) * weight
        )

    def take(s, h):
        s_hop(s, h).wait_recv()
        for n in range(2):
            merge(s, h, n)

    inputs[5].wait()
    for h in range(HEADS):
        first_block(h)

    @pl.when(is1)
    def _():
        for h in range(HEADS):
            wait_extra(h)
            attend(h, q_front[:, lanes[h]], [(k_ext[:, lanes[h]], v_ext[:, lanes[h]], at_home(me - 1))])

    @pl.when(visit1)
    def _():
        b_hop(0).wait_recv()

        @pl.when(has_prev2)
        def _():
            b_hop(1).start()

    def wait_share(h):
        v_share(h).wait_recv()
        k_share(h).wait_recv()

    def near(h):
        device = me - 2
        attend(
            h,
            q_home[:, lanes[h]],
            shards(h, at_home(device), at_home(device + 1 - 2 * core)),
        )
        attend(
            HEADS + h,
            q_vis[0, :, lanes[h]],
            shards(h, sent_along(0, 0), sent_along(0, 1)),
            fresh=True,
        )

    @pl.when(has_prev)
    def _():
        for h in range(HEADS):
            k_hop(h).wait_recv()
            k_share(h).start()

            @pl.when(feeds)
            def _():
                moved = dot_right(k_own[:, lanes[h]], chip_maps[h], NT)
                k_stage[1, :, lanes[h]] = moved.astype(bf16)
                k_extra(h, k_stage.at[1], cross).start()
                v_extra(h, v_own, cross).start()

            @pl.when(visit1)
            def _():
                q_hop(0, h).wait_recv()
                moved = dot_right(q_in[0, :, lanes[h]], chip_maps[h], NN)
                q_vis[0, :, lanes[h]] = moved.astype(bf16)

                @pl.when(has_prev2)
                def _():
                    q_hop(1, h).start()

            if h > 0:
                wait_share(h - 1)
                near(h - 1)
        wait_share(HEADS - 1)

    def far(h):
        @pl.when(visit2)
        def _():
            q_hop(1, h).wait_recv()
            moved = dot_right(q_in[1, :, lanes[h]], chip_maps[h], NN)
            q_vis[1, :, lanes[h]] = moved.astype(bf16)

            @pl.when(is0 & has_prev2)
            def _():
                wait_extra(h)

            attend(
                2 * HEADS + h,
                q_vis[1, :, lanes[h]],
                shards(h, sent_along(1, 2), sent_along(1, 3))
                + [(k_ext[:, lanes[h]], v_ext[:, lanes[h]], sent_along(1, 4))],
                fresh=True,
            )
            give(1, h)

    def back(h):
        @pl.when(visit1)
        def _():
            @pl.when(has_prev2)
            def _():
                take(1, h)

            give(0, h)

    @pl.when(visit2)
    def _():
        b_hop(1).wait_recv()

    far(0)
    far(1)
    far(2)

    @pl.when(has_prev)
    def _():
        near(HEADS - 1)

    for r in range(3):
        w_recv(r).wait_recv()
        w_share(r, half).start()
    back(0)
    far(3)
    back(1)
    back(2)

    def pass_head(h):
        a_hop(0, h, 0, x_left, x_left).wait_recv()
        a_relay(0, h, x_left, x_right).start()
        a_hop(1, h, 1, x_right, x_right).wait_recv()
        a_relay(1, h, x_right, x_left).start()

    def finish(h):
        for n in range(2):

            @pl.when(has_prev2)
            def _():
                if n == 0:
                    s_hop(0, h).wait_recv()
                merge(0, h, n)

            norm = jnp.sum(l_ref[h, rows[n], :], -1, keepdims=True)
            att[x, rows[n], lanes[h]] = (acc_ref[h, rows[n], :] / norm).astype(bf16)
            a_hop(0, h, n, x, x_right).start()
            a_hop(1, h, n, x, x_left).start()

    finish(0)
    back(3)
    finish(1)
    finish(2)
    pass_head(0)
    finish(3)
    pass_head(1)

    for r in range(3):
        w_share(r, other_half).wait_recv()
    own_w.wait()
    total = dot(att[x], wfull[x], NN)

    def near_part(total, h):
        a_hop(0, h, 1, x_left, x_left).wait_recv()
        a_hop(1, h, 0, x_right, x_right).wait_recv()
        for src in (x_left, x_right):
            total = total + dot(att[src, :, lanes[h]], wfull[src, lanes[h], :], NN)
        return total

    pass_head(2)
    pass_head(3)
    total = near_part(near_part(total, 0), 1)
    total = near_part(near_part(total, 2), 3)
    for h in range(HEADS):
        a_relay(0, h, x_far, x_left).wait_recv()
        a_relay(1, h, x_far, x_right).wait_recv()
        total = total + dot(att[x_far, :, lanes[h]], wfull[x_far, lanes[h], :], NN)
    out_ref[...] = total.astype(bf16)

    exchange_d.wait_send()
    for r in range(3):
        w_send(r).wait_send()
        w_share(r, half).wait_send()
    for h in range(HEADS):
        for part in range(2):
            a_hop(0, h, part, x, x_right).wait_send()
            a_hop(1, h, part, x, x_left).wait_send()
        a_relay(0, h, x_left, x_right).wait_send()
        a_relay(1, h, x_right, x_left).wait_send()

    @pl.when(has_next)
    def _():
        for h in range(HEADS):
            v_hop(h).wait_send()
            k_hop(h).wait_send()

    @pl.when(has_prev)
    def _():
        for h in range(HEADS):
            v_share(h).wait_send()
            k_share(h).wait_send()

    @pl.when(is0 | feeds)
    def _():
        for h in range(HEADS):
            v_extra(h, v_own, cross).wait_send()
            k_extra(h, k_tail, cross).wait_send()

    @pl.when(has_prev2)
    def _():
        b_hop(0).wait_send()
        for h in range(HEADS):
            q_hop(0, h).wait_send()

    @pl.when(visit1 & has_prev2)
    def _():
        b_hop(1).wait_send()
        for h in range(HEADS):
            q_hop(1, h).wait_send()

    for s, given in ((0, visit1), (1, visit2)):

        @pl.when(given)
        def _():
            for h in range(HEADS):
                for n in range(2):
                    o_hop(s, h, n).wait_send()
                s_hop(s, h).wait_send()


def solution(mesh):
    n_ctx = mesh.shape["ctx"]

    def body(queries, keys, values, directions, rates, selected, out_weight):
        tokens, width = queries.shape
        shard = (tokens, width)
        dma = pltpu.SemaphoreType.DMA
        vmem = pl.BlockSpec(memory_space=pltpu.VMEM)
        slab = pltpu.VMEM(shard, bf16)
        square = pltpu.VMEM((HD, width), f32)
        state = pltpu.VMEM((3 * HEADS, tokens, HD), f32)

        def pair(shape, dtype):
            return pltpu.VMEM((2,) + shape, dtype)

        scratch = [pltpu.SMEM(selected.shape, jnp.int32)] + [slab] * 4 + [pltpu.VMEM(rates.shape, f32)]
        scratch += [slab] * 6 + [pair(shard, bf16), slab, square, square]
        scratch += [slab, slab, pair(shard, bf16), pair(shard, bf16)]
        scratch += [pltpu.VMEM((20, HD), f32), pair((20, HD), f32)]
        scratch += [pair(shard, bf16), pair(shard, bf16)]
        scratch += [pair((HEADS, 2, HD), f32), pair((HEADS, 2, HD), f32)]
        scratch += [state, state, state, pltpu.VMEM((HEADS, tokens, tokens), f32)]
        scratch += [pltpu.VMEM((4,) + shard, bf16), pltpu.VMEM((4, width, width), bf16)]
        each, two, halves = (HEADS,), (2, HEADS), (2, HEADS, 2)
        sems = [each] * 12 + [(), (), two, two, (2,), (2,), halves, halves, two, two]
        sems += [(3,), (3,), (3,), (3,), halves, halves, two, two, (), (6,)]
        scratch += [dma(s) if s else dma for s in sems]
        return pl.pallas_call(
            functools.partial(kernel, n_ctx),
            out_shape=pltpu.VMEM(shard, bf16),
            in_specs=[
            ]
            + [pl.BlockSpec(memory_space=pl.ANY)] * 7,
            out_specs=vmem,
            scratch_shapes=scratch,
            compiler_params=pltpu.CompilerParams(
                collective_id=0, has_side_effects=True, vmem_limit_bytes=56 << 20
            ),
            name="path_attention",
        )(selected, queries, keys, values, directions, rates, out_weight)

    in_specs = (
        P("ctx", "head"),
        P("ctx", "head"),
        P("ctx", "head"),
        P("ctx", "head"),
        P("head", "ctx"),
        P("ctx", None),
        P("head", None),
    )
    return jax.shard_map(
        body, mesh=mesh, in_specs=in_specs, out_specs=P("ctx", "head"), check_vma=False
    )
```

```python
import functools

import jax
import jax.numpy as jnp
from jax import lax
from jax.experimental import pallas as pl
from jax.experimental.pallas import tpu as pltpu
from jax.sharding import PartitionSpec as P

MESH = pl.DeviceIdType.MESH
HD = 128
B = 128
HEADS = 4
NEG = -1e30
PAUSE_AT = 4
SCALE = HD ** (-0.5)
f32 = jnp.float32
bf16 = jnp.bfloat16
NN = (((1,), (0,)), ((), ()))
NT = (((1,), (1,)), ((), ()))
TN = (((0,), (0,)), ((), ()))


def dot(a, b, dims):
    return lax.dot_general(a, b, dims, preferred_element_type=f32)


def split(a):
    high = a.astype(bf16)
    return high, (a - high.astype(f32)).astype(bf16)


def dot3(a, b, dims):
    return dot(a[0], b[0], dims) + (dot(a[1], b[0], dims) + dot(a[0], b[1], dims))


def dot_left(a, b, dims):
    return dot(a[0], b, dims) + dot(a[1], b, dims)


def dot_right(a, b, dims):
    return dot(a, b[0], dims) + dot(a, b[1], dims)


def block_terms(q, k, w, beta, pause, pause_at):
    each = range(len(q))
    row = lax.broadcasted_iota(jnp.int32, (B, B), 0)
    col = lax.broadcasted_iota(jnp.int32, (B, B), 1)
    eye = (row == col).astype(f32)
    grams = [
        dot(jnp.concatenate([w[i], q[i]], 0), jnp.concatenate([w[i], k[i]], 0), NT) for i in each
    ]
    wide = [w[i].astype(f32) for i in each]
    norm = [jnp.sum(wide[i] * wide[i], -1, keepdims=True) for i in each]
    rate = [
        jnp.transpose(jnp.broadcast_to(beta[i], (B, B))) / (norm[i] + 1e-6) for i in each
    ]
    lower = [jnp.where(row > col, rate[i] * grams[i][:B, :B], 0.0) for i in each]
    key_proj = [split(jnp.where(row > col, grams[i][:B, B:], 0.0)) for i in each]
    query_proj = [split(jnp.where(row >= col, grams[i][B:, :B], 0.0)) for i in each]

    def off_diagonal(size):
        return ((row ^ col) < 2 * size) & ((row & size) != 0) & ((col & size) == 0)

    inverse = [eye - jnp.where(off_diagonal(1), lower[i], 0.0) for i in each]
    size = 2
    while size < B:
        mask = off_diagonal(size)
        parts = [split(inverse[i]) for i in each]
        below = [split(jnp.where(mask, lower[i], 0.0)) for i in each]
        step = [split(dot3(below[i], parts[i], NN)) for i in each]
        inverse = [inverse[i] - dot3(parts[i], step[i], NN) for i in each]
        if size == pause_at:
            pause()
        size *= 2
    mixing = [split(inverse[i] * jnp.transpose(rate[i])) for i in each]
    mix_w = [split(dot_left(mixing[i], w[i], NN)) for i in each]
    mix_k = [split(dot3(mixing[i], key_proj[i], NN)) for i in each]
    block_map = [eye - dot_right(w[i], mix_w[i], TN) for i in each]
    k_end = [k[i].astype(f32) - dot_left(mix_k[i], w[i], TN) for i in each]
    q_start = [q[i].astype(f32) - dot3(query_proj[i], mix_w[i], NN) for i in each]
    inner = [grams[i][B:, B:] - dot3(query_proj[i], mix_k[i], NN) for i in each]
    return q_start, k_end, inner, block_map


def kernel(
    n_ctx, sel_hbm, q_hbm, k_hbm, v_hbm, w_hbm, rate_hbm, ow_ref, out_ref,
    sel, q_ref, k_ref, v_ref, w_ref, rate_ref,
    k_own, k_par, k_ext, v_own, v_par, v_ext, k_stage, k_tail, d_mine, d_part,
    q_front, q_home, q_in, q_vis, b_mine, b_in, o_out, o_in, s_out, s_in,
    m_ref, l_ref, acc_ref, local, att, wfull,
    sv, rv, svp, rvp, sve, rve, sk, rk, skp, rkp, ske, rke, sd, rd, sq, rq, sb, rb, so, ro, ss, rs,
    sw, rw, swp, rwp, sa, ra, sar, rar, lw, li,
):
    me = lax.axis_index("ctx")
    x = lax.axis_index("head")
    core = lax.rem(me, 2)
    is0 = core == 0
    is1 = core == 1
    n_x = 4
    nxt = lax.rem(me + 2, n_ctx)
    prv = lax.rem(me + n_ctx - 2, n_ctx)
    partner = me + 1 - 2 * core
    cross = jnp.where(is0, lax.rem(me + n_ctx - 1, n_ctx), lax.rem(me + 1, n_ctx))
    x_right = lax.rem(x + 1, n_x)
    x_left = lax.rem(x + n_x - 1, n_x)
    x_far = lax.rem(x + 2, n_x)
    has_next = me + 2 < n_ctx
    has_next2 = me + 4 < n_ctx
    has_prev = me >= 2
    has_prev2 = me >= 4
    crossed = (is0 & has_prev) | (is1 & has_next)
    feeds = is1 & has_prev & (me + 6 < n_ctx)
    visit1 = has_prev & has_next
    visit2 = has_prev & has_next2
    lanes = [slice(h * HD, (h + 1) * HD) for h in range(HEADS)]
    rows = [slice(n * B, (n + 1) * B) for n in range(2)]

    def remote(src, dst, send, recv, to):
        return pltpu.make_async_remote_copy(
            src_ref=src, dst_ref=dst, send_sem=send, recv_sem=recv, device_id=to, device_id_type=MESH
        )

    barrier = pltpu.get_barrier_semaphore()
    for other, there in ((nxt, has_next), (prv, has_prev), (cross, crossed)):

        @pl.when(there)
        def _():
            pl.semaphore_signal(barrier, inc=1, device_id=(other, x), device_id_type=MESH)

    pl.semaphore_signal(barrier, inc=1, device_id=(partner, x), device_id_type=MESH)
    for other in (x_right, x_far, x_left):
        pl.semaphore_signal(barrier, inc=1, device_id=(me, other), device_id_type=MESH)
    count = lambda flag: jnp.where(flag, 1, 0)
    greetings = 4 + count(has_next) + count(has_prev) + count(crossed)
    inputs = [
        pltpu.make_async_copy(source, target, li.at[i])
        for i, (source, target) in enumerate(
            (
                (sel_hbm, sel), (w_hbm, w_ref), (k_hbm, k_ref), (q_hbm, q_ref),
                (rate_hbm, rate_ref), (v_hbm, v_ref),
            )
        )
    ]
    for copy in inputs:
        copy.start()

    def v_hop(h):
        return remote(v_hbm.at[:, lanes[h]], v_own.at[:, lanes[h]], sv.at[h], rv.at[h], (nxt, x))

    def k_hop(h):
        return remote(
            k_stage.at[0, :, lanes[h]], k_own.at[:, lanes[h]], sk.at[h], rk.at[h], (nxt, x)
        )

    def v_share(h):
        return remote(
            v_own.at[:, lanes[h]], v_par.at[:, lanes[h]], svp.at[h], rvp.at[h], (partner, x)
        )

    def k_share(h):
        return remote(
            k_own.at[:, lanes[h]], k_par.at[:, lanes[h]], skp.at[h], rkp.at[h], (partner, x)
        )

    def v_extra(h, src, to):
        return remote(src.at[:, lanes[h]], v_ext.at[:, lanes[h]], sve.at[h], rve.at[h], (to, x))

    def k_extra(h, src, to):
        return remote(src.at[:, lanes[h]], k_ext.at[:, lanes[h]], ske.at[h], rke.at[h], (to, x))

    def q_hop(s, h):
        src = q_home.at[:, lanes[h]] if s == 0 else q_vis.at[0, :, lanes[h]]
        return remote(src, q_in.at[s, :, lanes[h]], sq.at[s, h], rq.at[s, h], (prv, x))

    def b_hop(s):
        src = b_mine if s == 0 else b_in.at[0]
        return remote(src, b_in.at[s], sb.at[s], rb.at[s], (prv, x))

    def o_hop(s, h, n):
        return remote(
            o_out.at[s, rows[n], lanes[h]], o_in.at[s, rows[n], lanes[h]],
            so.at[s, h, n], ro.at[s, h, n], (nxt, x),
        )

    def s_hop(s, h, n):
        return remote(
            s_out.at[s, h, n], s_in.at[s, h, n], ss.at[s, h, n], rs.at[s, h, n], (nxt, x)
        )

    half = pl.ds(pl.multiple_of(core * 256, 256), 256)
    other_half = pl.ds(pl.multiple_of((1 - core) * 256, 256), 256)
    peers = [(x_right, x_left), (x_far, x_far), (x_left, x_right)]

    def w_send(r):
        to = peers[r][0]
        cols = pl.ds(pl.multiple_of(to * 512, 512), 512)
        return remote(ow_ref.at[half, cols], wfull.at[x, half], sw.at[r], rw.at[r], (me, to))

    def w_recv(r):
        src = peers[r][1]
        return remote(wfull.at[src, half], wfull.at[src, half], sw.at[r], rw.at[r], (me, src))

    def w_share(r, part):
        slot = wfull.at[peers[r][1], part]
        return remote(slot, slot, swp.at[r], rwp.at[r], (partner, x))

    def a_hop(r, h, part, owner, to):
        slot = att.at[owner, rows[part], lanes[h]]
        return remote(slot, slot, sa.at[r, h, part], ra.at[r, h, part], (me, to))

    def a_relay(r, h, owner, to):
        slot = att.at[owner, rows[r], lanes[h]]
        return remote(slot, slot, sar.at[r, h], rar.at[r, h], (me, to))

    own_w = pltpu.make_async_copy(
        ow_ref.at[:, pl.ds(pl.multiple_of(x * 512, 512), 512)], wfull.at[x], lw
    )

    def leave():
        pl.semaphore_wait(barrier, greetings)

        @pl.when(has_next)
        def _():
            for h in range(HEADS):
                v_hop(h).start()

        @pl.when(is0)
        def _():
            for h in range(HEADS):
                v_extra(h, v_hbm, partner).start()

        for r in range(3):
            w_send(r).start()
        own_w.start()

        @pl.when(has_prev2)
        def _():
            b_hop(0).start()

    def bias(n, block):
        hit = sel[n, 0] == block
        for e in range(1, 4):
            hit = hit | (sel[n, e] == block)
        return jnp.where(hit, 0.0, NEG).astype(f32)

    inputs[0].wait()
    away = [me - 4, me - 3 - 2 * core, me - 6, me - 5 - 2 * core, jnp.where(is0, me - 7, -1)]
    for n in range(2):
        for i, device in enumerate(away):
            for b in range(2):
                line = 10 * n + 2 * i + b
                b_mine[line : line + 1, :] = jnp.full((1, HD), bias(n, 2 * device + b), f32)

    @pl.when(is0 & (me < 4))
    def _():
        k_ext[...] = jnp.zeros_like(k_ext)
        v_ext[...] = jnp.zeros_like(v_ext)

    pairs = [(n, h) for h in range(HEADS) for n in range(2)]

    def cut(ref):
        return [ref[rows[n], lanes[h]] for n, h in pairs]

    for copy in inputs[1:5]:
        copy.wait()
    q_start, k_end, inner, block_map = block_terms(
        cut(q_ref), cut(k_ref), cut(w_ref), [rate_ref[h : h + 1, rows[n]] for n, h in pairs],
        leave, PAUSE_AT,
    )
    maps = [split(m) for m in block_map]
    tails, fronts = [], []
    for h in range(HEADS):
        d_mine[:, lanes[h]] = dot3(maps[2 * h + 1], maps[2 * h], NN)
    exchange_d = remote(d_mine, d_part, sd, rd, (partner, x))
    exchange_d.start()
    for h in range(HEADS):
        first, second = 2 * h, 2 * h + 1
        early = split(k_end[first])
        tails.append(jnp.concatenate([dot3(early, maps[second], NT), k_end[second]], 0))
        late = split(q_start[second])
        fronts.append(jnp.concatenate([q_start[first], dot3(late, maps[first], NN)], 0))
        q_front[:, lanes[h]] = (fronts[h] * SCALE).astype(bf16)
        k_tail[:, lanes[h]] = tails[h].astype(bf16)
        local[h, B:, :B] = dot3(late, early, NT) * SCALE
        local[h, :B, :B] = inner[first] * SCALE
        local[h, B:, B:] = inner[second] * SCALE

    @pl.when(is0)
    def _():
        for h in range(HEADS):
            k_extra(h, k_tail, partner).start()

    def pass_values(heads):
        @pl.when(has_prev)
        def _():
            for h in heads:
                v_hop(h).wait_recv()
                v_share(h).start()

    pass_values((0,))
    exchange_d.wait_recv()
    others = [split(d_part[:, lanes[h]]) for h in range(HEADS)]
    for h in range(HEADS):
        moved = dot3(split(fronts[h]), others[h], NN)
        q_home[:, lanes[h]] = (jnp.where(is0, fronts[h], moved) * SCALE).astype(bf16)

    @pl.when(has_prev2)
    def _():
        for h in range(HEADS):
            q_hop(0, h).start()

    for h in range(HEADS):
        carried = dot3(split(tails[h]), others[h], NT)
        k_stage[0, :, lanes[h]] = jnp.where(is0, carried, tails[h]).astype(bf16)

    @pl.when(has_next)
    def _():
        for h in range(HEADS):
            k_hop(h).start()

    chip_maps = []
    for h in range(HEADS):
        d_own = d_mine[:, lanes[h]]
        d_other = d_part[:, lanes[h]]
        later = jnp.where(is0, d_other, d_own)
        sooner = jnp.where(is0, d_own, d_other)
        chip_maps.append(split(dot3(split(later), split(sooner), NN)))
    pass_values((1, 2, 3))

    def first_block(h):
        row = lax.broadcasted_iota(jnp.int32, (B, B), 0)
        col = lax.broadcasted_iota(jnp.int32, (B, B), 1)
        for n in range(2):
            tiles = [local[h, rows[n], rows[b]] + bias(n, 2 * me + b) for b in range(n)]
            tiles.append(
                jnp.where(row >= col, local[h, rows[n], rows[n]] + bias(n, 2 * me + n), NEG)
            )
            top = functools.reduce(jnp.maximum, tiles)
            top = jnp.broadcast_to(jnp.max(top, -1, keepdims=True), (B, B))
            expos = [jnp.exp(t - top) for t in tiles]
            m_ref[h, rows[n], :] = top
            l_ref[h, rows[n], :] = functools.reduce(jnp.add, expos)
            total = jnp.zeros((B, HD), f32)
            for b, e in enumerate(expos):
                total = total + dot(e.astype(bf16), v_ref[rows[b], lanes[h]], NN)
            acc_ref[h, rows[n], :] = total

    def attend(g, query, sources, fresh=False):
        scores = [dot(query, keys, NT) for keys, _, _ in sources]
        for n in range(2):
            tiles = [
                scores[i][rows[n], rows[b]] + offset(n, b)
                for i, (_, _, offset) in enumerate(sources)
                for b in range(2)
            ]
            top = functools.reduce(jnp.maximum, tiles)
            top = jnp.broadcast_to(jnp.max(top, -1, keepdims=True), (B, B))
            if not fresh:
                old = m_ref[g, rows[n], :]
                top = jnp.maximum(old, top)
                fade = jnp.exp(old - top)
            expos = [jnp.exp(t - top) for t in tiles]
            norm = functools.reduce(jnp.add, expos)
            if not fresh:
                norm = norm + l_ref[g, rows[n], :] * fade
            m_ref[g, rows[n], :] = top
            l_ref[g, rows[n], :] = norm
            total = None if fresh else acc_ref[g, rows[n], :] * fade
            for i, (_, values, _) in enumerate(sources):
                weights = jnp.concatenate(expos[2 * i : 2 * i + 2], 1).astype(bf16)
                part = dot(weights, values, NN)
                total = part if total is None else total + part
            acc_ref[g, rows[n], :] = total

    def at_home(device):
        return lambda n, b: bias(n, 2 * device + b)

    def sent_along(s, i):
        def offset(n, b):
            line = 10 * n + 2 * i + b
            return b_in[s, line : line + 1, :]

        return offset

    def shards(h, own, other):
        return [
            (k_own[:, lanes[h]], v_own[:, lanes[h]], own),
            (k_par[:, lanes[h]], v_par[:, lanes[h]], other),
        ]

    def wait_extra(h):
        v_extra(h, v_own, cross).wait_recv()
        k_extra(h, k_tail, cross).wait_recv()

    def give_half(s, h, n):
        g = (s + 1) * HEADS + h
        norm = jnp.sum(l_ref[g, rows[n], :], -1, keepdims=True)
        o_out[s, rows[n], lanes[h]] = (acc_ref[g, rows[n], :] / norm).astype(bf16)
        s_out[s, h, n, :, :] = jnp.transpose(m_ref[g, rows[n], :] + jnp.log(norm))[:1, :]
        s_hop(s, h, n).start()
        o_hop(s, h, n).start()

    def give(s, h):
        for n in range(2):
            give_half(s, h, n)

    def merge(s, h, n):
        g = s * HEADS + h
        s_hop(s, h, n).wait_recv()
        o_hop(s, h, n).wait_recv()
        log = jnp.transpose(jnp.broadcast_to(s_in[s, h, n, :, :], (B, B)))
        old = m_ref[g, rows[n], :]
        top = jnp.maximum(old, log)
        fade, weight = jnp.exp(old - top), jnp.exp(log - top)
        m_ref[g, rows[n], :] = top
        l_ref[g, rows[n], :] = l_ref[g, rows[n], :] * fade + weight * (1.0 / B)
        acc_ref[g, rows[n], :] = (
            acc_ref[g, rows[n], :] * fade + o_in[s, rows[n], lanes[h]].astype(f32) * weight
        )

    inputs[5].wait()
    for h in range(HEADS):
        first_block(h)

    @pl.when(is1)
    def _():
        for h in range(HEADS):
            wait_extra(h)
            attend(h, q_front[:, lanes[h]], [(k_ext[:, lanes[h]], v_ext[:, lanes[h]], at_home(me - 1))])

    @pl.when(visit1)
    def _():
        b_hop(0).wait_recv()

        @pl.when(has_prev2)
        def _():
            b_hop(1).start()

    def wait_share(h):
        v_share(h).wait_recv()
        k_share(h).wait_recv()

    def near(h):
        device = me - 2
        attend(
            h,
            q_home[:, lanes[h]],
            shards(h, at_home(device), at_home(device + 1 - 2 * core)),
        )
        attend(
            HEADS + h,
            q_vis[0, :, lanes[h]],
            shards(h, sent_along(0, 0), sent_along(0, 1)),
            fresh=True,
        )

    @pl.when(has_prev)
    def _():
        for h in range(HEADS):
            k_hop(h).wait_recv()
            k_share(h).start()

            @pl.when(feeds)
            def _():
                moved = dot_right(k_own[:, lanes[h]], chip_maps[h], NT)
                k_stage[1, :, lanes[h]] = moved.astype(bf16)
                k_extra(h, k_stage.at[1], cross).start()
                v_extra(h, v_own, cross).start()

            @pl.when(visit1)
            def _():
                q_hop(0, h).wait_recv()
                moved = dot_right(q_in[0, :, lanes[h]], chip_maps[h], NN)
                q_vis[0, :, lanes[h]] = moved.astype(bf16)

                @pl.when(has_prev2)
                def _():
                    q_hop(1, h).start()

            if h > 0:
                wait_share(h - 1)
                near(h - 1)
        wait_share(HEADS - 1)

    def far(h):
        @pl.when(visit2)
        def _():
            q_hop(1, h).wait_recv()
            moved = dot_right(q_in[1, :, lanes[h]], chip_maps[h], NN)
            q_vis[1, :, lanes[h]] = moved.astype(bf16)

            @pl.when(is0 & has_prev2)
            def _():
                wait_extra(h)

            attend(
                2 * HEADS + h,
                q_vis[1, :, lanes[h]],
                shards(h, sent_along(1, 2), sent_along(1, 3))
                + [(k_ext[:, lanes[h]], v_ext[:, lanes[h]], sent_along(1, 4))],
                fresh=True,
            )
            give(1, h)

    def back(h):
        @pl.when(visit1)
        def _():
            for n in range(2):

                @pl.when(has_prev2)
                def _():
                    merge(1, h, n)

                give_half(0, h, n)

    @pl.when(visit2)
    def _():
        b_hop(1).wait_recv()

    far(0)
    far(1)
    far(2)

    @pl.when(has_prev)
    def _():
        near(HEADS - 1)

    for r in range(3):
        w_recv(r).wait_recv()
        w_share(r, half).start()
    back(0)
    far(3)
    back(1)
    back(2)

    def pass_head(h):
        a_hop(0, h, 0, x_left, x_left).wait_recv()
        a_relay(0, h, x_left, x_right).start()
        a_hop(1, h, 1, x_right, x_right).wait_recv()
        a_relay(1, h, x_right, x_left).start()

    def finish(h):
        for n in range(2):

            @pl.when(has_prev2)
            def _():
                merge(0, h, n)

            norm = jnp.sum(l_ref[h, rows[n], :], -1, keepdims=True)
            att[x, rows[n], lanes[h]] = (acc_ref[h, rows[n], :] / norm).astype(bf16)
            a_hop(0, h, n, x, x_right).start()
            a_hop(1, h, n, x, x_left).start()

    finish(0)
    back(3)
    finish(1)
    finish(2)
    pass_head(0)
    finish(3)
    pass_head(1)

    for r in range(3):
        w_share(r, other_half).wait_recv()
    own_w.wait()
    total = dot(att[x], wfull[x], NN)

    def near_part(total, h):
        a_hop(0, h, 1, x_left, x_left).wait_recv()
        a_hop(1, h, 0, x_right, x_right).wait_recv()
        for src in (x_left, x_right):
            total = total + dot(att[src, :, lanes[h]], wfull[src, lanes[h], :], NN)
        return total

    pass_head(2)
    pass_head(3)
    total = near_part(near_part(total, 0), 1)
    total = near_part(near_part(total, 2), 3)
    for h in range(HEADS):
        a_relay(0, h, x_far, x_left).wait_recv()
        a_relay(1, h, x_far, x_right).wait_recv()
        total = total + dot(att[x_far, :, lanes[h]], wfull[x_far, lanes[h], :], NN)
    out_ref[...] = total.astype(bf16)

    exchange_d.wait_send()
    for r in range(3):
        w_send(r).wait_send()
        w_share(r, half).wait_send()
    for h in range(HEADS):
        for part in range(2):
            a_hop(0, h, part, x, x_right).wait_send()
            a_hop(1, h, part, x, x_left).wait_send()
        a_relay(0, h, x_left, x_right).wait_send()
        a_relay(1, h, x_right, x_left).wait_send()

    @pl.when(has_next)
    def _():
        for h in range(HEADS):
            v_hop(h).wait_send()
            k_hop(h).wait_send()

    @pl.when(has_prev)
    def _():
        for h in range(HEADS):
            v_share(h).wait_send()
            k_share(h).wait_send()

    @pl.when(is0 | feeds)
    def _():
        for h in range(HEADS):
            v_extra(h, v_own, cross).wait_send()
            k_extra(h, k_tail, cross).wait_send()

    @pl.when(has_prev2)
    def _():
        b_hop(0).wait_send()
        for h in range(HEADS):
            q_hop(0, h).wait_send()

    @pl.when(visit1 & has_prev2)
    def _():
        b_hop(1).wait_send()
        for h in range(HEADS):
            q_hop(1, h).wait_send()

    for s, given in ((0, visit1), (1, visit2)):

        @pl.when(given)
        def _():
            for h in range(HEADS):
                for n in range(2):
                    o_hop(s, h, n).wait_send()
                for n in range(2):
                    s_hop(s, h, n).wait_send()


def solution(mesh):
    n_ctx = mesh.shape["ctx"]

    def body(queries, keys, values, directions, rates, selected, out_weight):
        tokens, width = queries.shape
        shard = (tokens, width)
        dma = pltpu.SemaphoreType.DMA
        vmem = pl.BlockSpec(memory_space=pltpu.VMEM)
        slab = pltpu.VMEM(shard, bf16)
        square = pltpu.VMEM((HD, width), f32)
        state = pltpu.VMEM((3 * HEADS, tokens, HD), f32)

        def pair(shape, dtype):
            return pltpu.VMEM((2,) + shape, dtype)

        scratch = [pltpu.SMEM(selected.shape, jnp.int32)] + [slab] * 4 + [pltpu.VMEM(rates.shape, f32)]
        scratch += [slab] * 6 + [pair(shard, bf16), slab, square, square]
        scratch += [slab, slab, pair(shard, bf16), pair(shard, bf16)]
        scratch += [pltpu.VMEM((20, HD), f32), pair((20, HD), f32)]
        scratch += [pair(shard, bf16), pair(shard, bf16)]
        scratch += [pair((HEADS, 2, 1, HD), f32), pair((HEADS, 2, 1, HD), f32)]
        scratch += [state, state, state, pltpu.VMEM((HEADS, tokens, tokens), f32)]
        scratch += [pltpu.VMEM((4,) + shard, bf16), pltpu.VMEM((4, width, width), bf16)]
        each, two, halves = (HEADS,), (2, HEADS), (2, HEADS, 2)
        sems = [each] * 12 + [(), (), two, two, (2,), (2,), halves, halves, halves, halves]
        sems += [(3,), (3,), (3,), (3,), halves, halves, two, two, (), (6,)]
        scratch += [dma(s) if s else dma for s in sems]
        return pl.pallas_call(
            functools.partial(kernel, n_ctx),
            out_shape=pltpu.VMEM(shard, bf16),
            in_specs=[
            ]
            + [pl.BlockSpec(memory_space=pl.ANY)] * 7,
            out_specs=vmem,
            scratch_shapes=scratch,
            compiler_params=pltpu.CompilerParams(
                collective_id=0, has_side_effects=True, vmem_limit_bytes=56 << 20
            ),
            name="path_attention",
        )(selected, queries, keys, values, directions, rates, out_weight)

    in_specs = (
        P("ctx", "head"),
        P("ctx", "head"),
        P("ctx", "head"),
        P("ctx", "head"),
        P("head", "ctx"),
        P("ctx", None),
        P("head", None),
    )
    return jax.shard_map(
        body, mesh=mesh, in_specs=in_specs, out_specs=P("ctx", "head"), check_vma=False
    )
```
